32 devices in a mesh: dom: 8 (over y, x, core), section: 4 (over z).
Axes of the slice: x: 2, y: 2, z: 4, core: 2. Of those that a mesh axis runs over, the one named last changes fastest.
Arguments:
- saved_inputs: bfloat16 [4, 4, 2048, 256], P('section', None, 'dom'), may hold values from -6 to 6
- grad_out: bfloat16 [4, 2048, 256], P(None, 'dom'), may hold values from -6 to 6
- w_first: bfloat16 [4, 512, 256], P('section'), may hold values from -0.25 to 0.25
- w_second: bfloat16 [4, 256, 256], P('section'), may hold values from -0.25 to 0.25
- face_weight: float32 [6, 2048], P(None, 'dom'), may hold values from 0.25 to 1
- neighbours: int32 [6, 2048], P(None, 'dom'), may hold values from 0 to 320, as said below
- send_rows: int32 [2, 256], P(None, 'dom'), may hold values from 0 to 255, as said below
Outputs:
- grad_in: bfloat16 [4, 4, 2048, 256], P('section', None, 'dom')
- grad_first: float32 [4, 512, 256], P('section')
- grad_second: float32 [4, 256, 256], P('section')
The draws below stay inside these ranges and needn't reach their ends.
Inputs may be any that keep to these rules, and one draw needn't show every extreme that they name: `neighbours`: slots count as: 0 to 31 the halo from below, 32 to 287 the partition's own cells, then 32 halo slots from above, and 320 a zero row for walls. A partition uses its halo slots unevenly; some partition uses all of them on both sides. `send_rows`: within one partition and one side the rows are distinct local row numbers.
All inputs are finite; a program needn't handle non-finite values.
Results may differ from the reference program's by a relative error of at most 0.027.
Values may be sent and summed in bfloat16 or wider, within the bound.
No kernel may reach another device: no remote copies, remote signals or barrier semaphores. Data moves between devices by JAX's collectives and lax.ppermute only.
A program may use at most 64 MiB of HBM per device.

```python
import math
import jax
import jax.numpy as jnp
from jax import lax

D = 256
K = 6
R = 256
M = 4
HB = 32
LAYERS = 4
CELLS = 2048


def draw_neighbours(key, part):
    parts = CELLS // R
    key_live, key_offset, key_wall = jax.random.split(key, 3)
    live = jax.random.randint(key_live, (2, parts), HB // 4, HB + 1)
    live = live.at[:, 1 % parts].set(HB)
    offsets = jax.random.randint(key_offset, (K, parts, R), -24, 25)
    cell = jnp.arange(R, dtype=jnp.int32)
    local = jnp.clip(cell[None, None, :] + offsets, 0, R - 1) + HB
    wall = jax.random.randint(key_wall, (K, parts, R), 0, 12) == 0
    local = jnp.where(wall, 2 * HB + R, local)
    below_use = cell[None, :] < live[0][:, None]
    above_use = (R - 1 - cell)[None, :] < live[1][:, None]
    above_index = HB + R + (R - 1 - cell)
    face_zero = jnp.where(below_use, cell[None, :], local[0])
    face_one = jnp.where(above_use, above_index[None, :], local[1])
    result = local.at[0].set(face_zero).at[1].set(face_one)
    result = result.at[2, :, 0].set(2 * HB + R)
    return result.reshape(K, parts * R).astype(jnp.int32)


def draw_send_rows(key, part):
    parts = CELLS // R
    keys = jax.random.split(key, 2 * parts + 1)

    def one_list(single):
        return jax.random.permutation(single, R)[:HB]
    rows = jax.vmap(one_list)(keys[:2 * parts])
    middle = jax.random.permutation(keys[2 * parts], R - 2)[:HB - 2] + 1
    ends = jnp.array([0, R - 1], dtype=jnp.int32)
    first = jnp.concatenate([ends[:1], middle.astype(jnp.int32), ends[1:]])
    rows = rows.astype(jnp.int32).at[0].set(first)
    return rows.reshape(2, parts * HB).astype(jnp.int32)


def block_scale(stream_key, dims, pieces, low, high):
    gain = 1.0
    for dim, blocks in pieces:
        steps = jax.random.uniform(jax.random.fold_in(jax.random.fold_in(stream_key, 6), dim), (blocks,), jnp.float32, low / len(pieces), high / len(pieces))
        gain = gain * jnp.repeat(jnp.exp(steps), dims[dim] // blocks).reshape((-1,) + (1,) * (len(dims) - 1 - dim))
    return gain


def bell_draw(own_key, dims, scale, bound, shards=(), kind=jnp.bfloat16):
    values = scale * jax.random.normal(own_key, dims, jnp.float32)
    if shards:
        values = values * block_scale(own_key, dims, shards, -0.22, 0.18)
    return jnp.clip(values, -bound, bound).astype(kind)


def setup_inputs(seed: int = 0) -> dict:
    key_of = jax.random.split(jax.random.key(seed), 8)
    return {
        "saved_inputs": bell_draw(key_of[0], (LAYERS, M, CELLS, D), 1.0, 6.0, ((0, 4), (2, 8))),
        "grad_out": bell_draw(key_of[1], (M, CELLS, D), 1.0, 6.0, ((1, 8),)),
        "w_first": bell_draw(key_of[2], (LAYERS, 2 * D, D), (2 * D) ** -0.5, 0.25, ((0, 4),)),
        "w_second": bell_draw(key_of[3], (LAYERS, D, D), (2 * D) ** -0.5, 0.25, ((0, 4),)),
        "face_weight": jnp.clip(jnp.exp(math.log(1.0) - 1.3862944 * jax.random.uniform(key_of[4], (K, CELLS), jnp.float32) ** block_scale(key_of[4], (K, CELLS), ((1, 8),), -0.2, 0.2)), 0.25, 1.0),
        "neighbours": draw_neighbours(jax.random.fold_in(key_of[7], 71), 0),
        "send_rows": draw_send_rows(jax.random.fold_in(key_of[7], 71), 0),
    }


def forward_part(x, below, above, nbr, coef, w_one):
    zero = jnp.zeros((x.shape[0], 1, x.shape[2]), x.dtype)
    ext = jnp.concatenate([below, x, above, zero], axis=1)
    rows = jnp.take(ext, nbr, axis=1)
    agg = jnp.sum(rows.astype(jnp.float32) * coef[None, :, :, None], axis=1).astype(jnp.bfloat16)
    joined = jnp.concatenate([x, agg], axis=2)
    z = jnp.einsum('mrj,jd->mrd', joined.astype(jnp.float32), w_one.astype(jnp.float32))
    act = jax.nn.silu(z).astype(jnp.bfloat16)
    return joined, z, act


def backward_part(joined, z, act, g, nbr, coef, w_one, w_two):
    width = g.shape[-1]
    rows = g.shape[1]
    slots = (nbr.shape[1]) // 8
    d_act = jnp.einsum('mrd,jd->mrj', g.astype(jnp.float32), w_two.astype(jnp.float32))
    sig = jax.nn.sigmoid(z)
    dz = (d_act * sig * (1.0 + z * (1.0 - sig))).astype(jnp.bfloat16)
    dw_two = jnp.einsum('mri,mrj->ij', act.astype(jnp.float32), g.astype(jnp.float32))
    dw_one = jnp.einsum('mri,mrj->ij', joined.astype(jnp.float32), dz.astype(jnp.float32))
    d_joined = jnp.einsum('mrj,ij->mri', dz.astype(jnp.float32), w_one.astype(jnp.float32))
    dx = d_joined[..., :width]
    dagg = d_joined[..., width:]
    contrib = dagg[:, None] * coef[None, :, :, None]
    flat = contrib.transpose(1, 2, 0, 3).reshape(-1, g.shape[0], width)
    dext = jax.ops.segment_sum(flat, nbr.reshape(-1), num_segments=rows + 2 * slots + 1)
    dext = dext.transpose(1, 0, 2)
    local = dx + dext[:, slots:slots + rows]
    return local, dext[:, :slots], dext[:, slots + rows:slots + rows + slots], dw_one, dw_two


def reference(saved_inputs, grad_out, w_first, w_second, face_weight, neighbours, send_rows):
    parts = CELLS // R
    coef = face_weight.reshape(K, parts, R).transpose(1, 0, 2)
    nbr = neighbours.reshape(K, parts, R).transpose(1, 0, 2)
    sends = send_rows.reshape(2, parts, HB).transpose(1, 0, 2)
    g = grad_out
    grads_in = [None] * LAYERS
    firsts = [None] * LAYERS
    seconds = [None] * LAYERS
    for layer in reversed(range(LAYERS)):
        x = saved_inputs[layer].reshape(M, parts, R, D).transpose(1, 0, 2, 3)
        up = jax.vmap(lambda xp, s: jnp.take(xp, s[0], axis=1))(x, sends)
        down = jax.vmap(lambda xp, s: jnp.take(xp, s[1], axis=1))(x, sends)
        zero = jnp.zeros_like(up[:1])
        below = jnp.concatenate([zero, up[:-1]], axis=0)
        above = jnp.concatenate([down[1:], zero], axis=0)
        gp = g.reshape(M, parts, R, D).transpose(1, 0, 2, 3)
        w_one = w_first[layer]
        w_two = w_second[layer]

        def one(item):
            xp, bp, ap, gpp, nb, cf = item
            joined, z, act = forward_part(xp, bp, ap, nb, cf, w_one)
            return backward_part(joined, z, act, gpp, nb, cf, w_one, w_two)

        local, slot_below, slot_above, dw1, dw2 = lax.map(one, (x, below, above, gp, nbr, coef))
        zero_slots = jnp.zeros_like(slot_below[:1])
        from_upper = jnp.concatenate([slot_below[1:], zero_slots], axis=0)
        from_lower = jnp.concatenate([zero_slots, slot_above[:-1]], axis=0)

        def place(loc, fu, fl, s):
            return loc.at[:, s[0]].add(fu).at[:, s[1]].add(fl)

        total = jax.vmap(place)(local, from_upper, from_lower, sends)
        g_new = (gp.astype(jnp.float32) + total).astype(jnp.bfloat16)
        g = g_new.transpose(1, 0, 2, 3).reshape(M, CELLS, D)
        grads_in[layer] = g
        firsts[layer] = jnp.sum(dw1, axis=0)
        seconds[layer] = jnp.sum(dw2, axis=0)
    return jnp.stack(grads_in), jnp.stack(firsts), jnp.stack(seconds)
```

```python
import jax
import jax.numpy as jnp
from jax import lax
from jax.experimental import pallas as pl
from jax.experimental.pallas import tpu as pltpu
from jax.sharding import PartitionSpec as P

F32 = jnp.float32
BF16 = jnp.bfloat16
CHUNKS = 2


def dot(a, b, dims=((1,), (0,))):
    return lax.dot_general(a, b, (dims, ((), ())), preferred_element_type=F32)


def vmem():
    return pl.BlockSpec(memory_space=pltpu.VMEM)


def params():
    return pltpu.CompilerParams(vmem_limit_bytes=48 * 1024 * 1024)


def pack_kernel(x_ref, send_ref, place_ref, up_ref, down_ref):
    batches, rows, _ = x_ref.shape
    slots = send_ref.shape[1]
    row = lax.broadcasted_iota(jnp.int32, (rows, slots), 0)
    up = jnp.where(row == send_ref[0:1, :], 1.0, 0.0)
    down = jnp.where(row == send_ref[1:2, :], 1.0, 0.0)
    place = jnp.concatenate([up, down], axis=1)
    place_ref[...] = place.astype(BF16)
    pick = place.T.astype(BF16)
    for m in range(batches):
        sent = dot(pick, x_ref[m]).astype(BF16)
        up_ref[m] = sent[:slots]
        down_ref[m] = sent[slots:]


def forward_kernel(x_ref, below_ref, above_ref, nbr_ref, coef_ref, w_ref,
                   slope_ref, act_ref, agg_ref, own_ref, halo_ref):
    batches, rows, width = x_ref.shape
    slots = below_ref.shape[1]
    faces = nbr_ref.shape[0]
    slot = lax.broadcasted_iota(jnp.int32, (rows + 2 * slots, rows), 0)
    spread = jnp.zeros((rows + 2 * slots, rows), F32)
    for k in range(faces):
        spread = spread + jnp.where(slot == nbr_ref[k : k + 1, :], coef_ref[k : k + 1, :], 0.0)
    own = spread[slots : slots + rows]
    halo = jnp.concatenate([spread[:slots], spread[slots + rows :]], axis=0)
    own_ref[...] = own.astype(BF16)
    halo_ref[...] = halo.astype(BF16)
    own_t = own.T.astype(BF16)
    halo_t = halo.T.astype(BF16)
    for m in range(batches):
        x = x_ref[m]
        edge = jnp.concatenate([below_ref[m], above_ref[m]], axis=0)
        agg = (dot(own_t, x) + dot(halo_t, edge)).astype(BF16)
        z = dot(x, w_ref[:width]) + dot(agg, w_ref[width:])
        sig = 1.0 / (1.0 + jnp.exp(-z))
        agg_ref[m] = agg
        act_ref[m] = (z * sig).astype(BF16)
        slope_ref[m] = sig * (1.0 + z * (1.0 - sig))


def layer_step(g, first, slope_ref, own_ref, halo_ref, w1_ref, w2_ref, sent, kept, g_buf, dz_buf, sems):
    rows, width = slope_ref.shape[1], slope_ref.shape[2]
    local_ref, below_ref, above_ref = sent
    slots = below_ref.shape[1]
    count = len(g)
    copies = []

    def keep(n, source):
        copy = pltpu.make_async_copy(source, kept[n].at[pl.ds(first, count)], sems.at[n])
        copy.start()
        copies.append(copy)

    for j in range(count):
        g_buf[j] = g[j]
    keep(3, g_buf)
    stacked = jnp.concatenate(g, axis=0) if count > 1 else g[0]
    d_act = dot(stacked, w2_ref[...], ((1,), (1,)))
    dzs = []
    for j in range(count):
        dz = (d_act[j * rows : (j + 1) * rows] * slope_ref[first + j]).astype(BF16)
        dz_buf[j] = dz
        dzs.append(dz)
    keep(4, dz_buf)
    dz = jnp.concatenate(dzs, axis=0) if count > 1 else dzs[0]
    dj = dot(dz, w1_ref[...], ((1,), (1,)))
    for j in range(count):
        part = dj[j * rows : (j + 1) * rows]
        dagg = part[:, width:].astype(BF16)
        local = g[j].astype(F32) + part[:, :width] + dot(own_ref[...], dagg)
        local_ref[j] = local.astype(BF16)
        edge = dot(halo_ref[...], dagg).astype(BF16)
        below_ref[j] = edge[:slots]
        above_ref[j] = edge[slots:]
    for n in range(3):
        keep(n, sent[n])
    for copy in copies:
        copy.wait()


def assemble(local, upper, lower, place):
    edge = jnp.concatenate([upper, lower], axis=0)
    return (local.astype(F32) + dot(place, edge)).astype(BF16)


def make_step_kernel(hop, first, count, fresh):
    def body(hop_ref, *refs):
        inputs, refs = (refs[:1], refs[1:]) if hop == 0 else (refs[:4], refs[4:])
        slope_ref, own_ref, halo_ref, w1_ref, w2_ref = refs[:5]
        refs = refs[5:] if fresh else refs[10:]
        sent, kept, (g_buf, dz_buf, sems) = refs[:3], refs[3:8], refs[8:]

        @pl.when(hop_ref[0] == hop)
        def _():
            if hop == 0:
                g = [inputs[0][first + j] for j in range(count)]
            else:
                loc_ref, upper_ref, lower_ref, place_ref = inputs
                g = [assemble(loc_ref[j], upper_ref[j], lower_ref[j], place_ref[...]) for j in range(count)]
            layer_step(g, first, slope_ref, own_ref, halo_ref, w1_ref, w2_ref, sent, kept, g_buf, dz_buf, sems)

    return body


def weight_kernel(x_ref, agg_ref, act_ref, g_ref, dz_ref, grad_ref):
    batches, rows, width = x_ref.shape
    total = batches * rows
    g = g_ref[...].reshape(total, width)
    dz = dz_ref[...].reshape(total, width)
    over = ((0,), (0,))
    grad_ref[:width] = dot(x_ref[...].reshape(total, width), dz, over)
    grad_ref[width : 2 * width] = dot(agg_ref[...].reshape(total, width), dz, over)
    grad_ref[2 * width :] = dot(act_ref[...].reshape(total, width), g, over)


def finish_kernel(loc_ref, upper_ref, lower_ref, place_ref, out_ref):
    for m in range(loc_ref.shape[0]):
        out_ref[m] = assemble(loc_ref[m], upper_ref[m], lower_ref[m], place_ref[...])


def sum_over_dom(part, count):
    if count & (count - 1) or count < 4:
        return lax.psum(part, "dom")
    me = lax.axis_index("dom")

    def swap(value, mask):
        return lax.ppermute(value, "dom", [(i, i ^ mask) for i in range(count)])

    half = part.shape[0] // 2
    low = me % 2 == 0
    keep = jnp.where(low, part[:half], part[half:])
    give = jnp.where(low, part[half:], part[:half]).astype(BF16)
    acc = keep + swap(give, 1).astype(F32)
    bit = 2
    while bit < count:
        mine = acc.astype(BF16)
        if bit * 2 < count:
            others = [swap(mine, mask) for mask in (bit, 2 * bit, 3 * bit)]
            a, b, c = [other.astype(F32) for other in others]
            acc = (mine.astype(F32) + a) + (b + c)
            bit *= 4
        else:
            acc = mine.astype(F32) + swap(mine, bit).astype(F32)
            bit *= 2
    mine = acc.astype(BF16)
    other = swap(mine, 1)
    first = jnp.where(low, mine, other)
    second = jnp.where(low, other, mine)
    return jnp.concatenate([first, second], axis=0).astype(F32)


def per_device(saved_inputs, grad_out, w_first, w_second, face_weight, neighbours, send_rows):
    x = saved_inputs[0]
    w1 = w_first[0]
    w2 = w_second[0]
    batches, rows, width = x.shape
    slots = send_rows.shape[1]
    sections = lax.axis_size("section")
    doms = lax.axis_size("dom")
    chunks = CHUNKS if batches % CHUNKS == 0 else 1
    count = batches // chunks
    hop_here = (sections - 1 - lax.axis_index("section")).astype(jnp.int32).reshape(1)
    sds = jax.ShapeDtypeStruct

    place, up, down = pl.pallas_call(
        pack_kernel,
        out_shape=(sds((rows, 2 * slots), BF16), sds((batches, slots, width), BF16),
                   sds((batches, slots, width), BF16)),
        compiler_params=params(), name="pack",
    )(x, send_rows)
    rise = [(i, i + 1) for i in range(doms - 1)]
    fall = [(i + 1, i) for i in range(doms - 1)]
    below = lax.ppermute(up, "dom", rise)
    above = lax.ppermute(down, "dom", fall)

    slope, act, agg, own, halo = pl.pallas_call(
        forward_kernel,
        out_shape=(sds((batches, rows, width), F32), sds((batches, rows, width), BF16),
                   sds((batches, rows, width), BF16), sds((rows, rows), BF16), sds((2 * slots, rows), BF16)),
        compiler_params=params(), name="forward",
    )(x, below, above, neighbours, face_weight, w1)

    def move(value, hop, shift):
        source = sections - 1 - hop
        pairs = [(p * sections + source, (p + shift) * sections + source - 1)
                 for p in range(doms) if 0 <= p + shift < doms]
        return lax.ppermute(value, ("dom", "section"), pairs)

    def shapes(n):
        full, edge = sds((n, rows, width), BF16), sds((n, slots, width), BF16)
        return (full, edge, edge)

    any_spec = pl.BlockSpec(memory_space=pl.ANY)
    kept = ()
    received = [None] * chunks
    for hop in range(sections):
        sent = []
        for c in range(chunks):
            inputs = (grad_out,) if hop == 0 else (*received[c], place)
            inputs = (hop_here, *inputs, slope, own, halo, w1, w2)
            outs = pl.pallas_call(
                make_step_kernel(hop, c * count, count, not kept),
                in_specs=[pl.BlockSpec(memory_space=pltpu.SMEM)] + [vmem()] * (len(inputs) - 1)
                + [any_spec] * len(kept),
                out_specs=[vmem()] * 3 + [any_spec] * 5,
                out_shape=shapes(count) + shapes(batches) + (shapes(batches)[0],) * 2,
                scratch_shapes=[pltpu.VMEM((count, rows, width), BF16), pltpu.VMEM((count, rows, width), BF16),
                                pltpu.SemaphoreType.DMA((5,))],
                input_output_aliases={len(inputs) + n: 3 + n for n in range(len(kept))},
                compiler_params=params(), name="step",
            )(*inputs, *kept)
            kept = outs[3:]
            if hop + 1 < sections:
                local, to_below, to_above = outs[:3]
                sent.append((move(local, hop, 0), move(to_below, hop, -1), move(to_above, hop, 1)))
        received = sent
    local, to_below, to_above, g, dz = kept

    grad = pl.pallas_call(
        weight_kernel, out_shape=sds((3 * width, width), F32),
        compiler_params=params(), name="weights",
    )(x, agg, act, g, dz)

    total = sum_over_dom(grad, doms)
    from_upper = lax.ppermute(to_below, "dom", fall)
    from_lower = lax.ppermute(to_above, "dom", rise)
    grad_in = pl.pallas_call(
        finish_kernel, out_shape=sds((batches, rows, width), BF16),
        compiler_params=params(), name="finish",
    )(local, from_upper, from_lower, place)
    return grad_in[None], total[None, : 2 * width], total[None, 2 * width :]


def solution(mesh):
    return jax.shard_map(
        per_device,
        mesh=mesh,
        in_specs=(
            P("section", None, "dom", None),
            P(None, "dom", None),
            P("section", None, None),
            P("section", None, None),
            P(None, "dom"),
            P(None, "dom"),
            P(None, "dom"),
        ),
        out_specs=(
            P("section", None, "dom", None),
            P("section", None, None),
            P("section", None, None),
        ),
        check_vma=False,
    )
```

```python
import jax
import jax.numpy as jnp
from jax import lax
from jax.experimental import pallas as pl
from jax.experimental.pallas import tpu as pltpu
from jax.sharding import PartitionSpec as P

F32 = jnp.float32
BF16 = jnp.bfloat16
CHUNKS = 2
STEP_FLOPS = 10**11


def dot(a, b, dims=((1,), (0,))):
    return lax.dot_general(a, b, (dims, ((), ())), preferred_element_type=F32)


def vmem():
    return pl.BlockSpec(memory_space=pltpu.VMEM)


def params():
    return pltpu.CompilerParams(vmem_limit_bytes=16 * 1024 * 1024)


def pack_kernel(x_ref, send_ref, place_ref, up_ref, down_ref):
    batches, rows, _ = x_ref.shape
    slots = send_ref.shape[1]
    row = lax.broadcasted_iota(jnp.int32, (rows, slots), 0)
    up = jnp.where(row == send_ref[0:1, :], 1.0, 0.0)
    down = jnp.where(row == send_ref[1:2, :], 1.0, 0.0)
    place = jnp.concatenate([up, down], axis=1)
    place_ref[...] = place.astype(BF16)
    pick = place.T.astype(BF16)
    for m in range(batches):
        sent = dot(pick, x_ref[m]).astype(BF16)
        up_ref[m] = sent[:slots]
        down_ref[m] = sent[slots:]


def forward_kernel(x_ref, below_ref, above_ref, nbr_ref, coef_ref, w_ref,
                   slope_ref, act_ref, agg_ref, own_ref, halo_ref):
    batches, rows, width = x_ref.shape
    slots = below_ref.shape[1]
    faces = nbr_ref.shape[0]
    slot = lax.broadcasted_iota(jnp.int32, (rows + 2 * slots, rows), 0)
    spread = jnp.zeros((rows + 2 * slots, rows), F32)
    for k in range(faces):
        spread = spread + jnp.where(slot == nbr_ref[k : k + 1, :], coef_ref[k : k + 1, :], 0.0)
    own = spread[slots : slots + rows]
    halo = jnp.concatenate([spread[:slots], spread[slots + rows :]], axis=0)
    own_ref[...] = own.astype(BF16)
    halo_ref[...] = halo.astype(BF16)
    own_t = own.T.astype(BF16)
    halo_t = halo.T.astype(BF16)
    for m in range(batches):
        x = x_ref[m]
        edge = jnp.concatenate([below_ref[m], above_ref[m]], axis=0)
        agg = (dot(own_t, x) + dot(halo_t, edge)).astype(BF16)
        z = dot(x, w_ref[:width]) + dot(agg, w_ref[width:])
        sig = 1.0 / (1.0 + jnp.exp(-z))
        agg_ref[m] = agg
        act_ref[m] = (z * sig).astype(BF16)
        slope_ref[m] = sig * (1.0 + z * (1.0 - sig))


def layer_step(g, first, slope_ref, own_ref, halo_ref, w1_ref, w2_ref, sent, kept, g_buf, dz_buf, sems):
    rows, width = slope_ref.shape[1], slope_ref.shape[2]
    local_ref, below_ref, above_ref = sent
    slots = below_ref.shape[1]
    count = len(g)
    copies = []

    def keep(n, source):
        copy = pltpu.make_async_copy(source, kept[n].at[pl.ds(first, count)], sems.at[n])
        copy.start()
        copies.append(copy)

    for j in range(count):
        g_buf[j] = g[j]
    keep(3, g_buf)
    stacked = jnp.concatenate(g, axis=0) if count > 1 else g[0]
    d_act = dot(stacked, w2_ref[...], ((1,), (1,)))
    dzs = []
    for j in range(count):
        dz = (d_act[j * rows : (j + 1) * rows] * slope_ref[first + j]).astype(BF16)
        dz_buf[j] = dz
        dzs.append(dz)
    keep(4, dz_buf)
    dz = jnp.concatenate(dzs, axis=0) if count > 1 else dzs[0]
    dj = dot(dz, w1_ref[...], ((1,), (1,)))
    for j in range(count):
        part = dj[j * rows : (j + 1) * rows]
        dagg = part[:, width:].astype(BF16)
        local = g[j].astype(F32) + part[:, :width] + dot(own_ref[...], dagg)
        local_ref[j] = local.astype(BF16)
        edge = dot(halo_ref[...], dagg).astype(BF16)
        below_ref[j] = edge[:slots]
        above_ref[j] = edge[slots:]
    for n in range(3):
        keep(n, sent[n])
    for copy in copies:
        copy.wait()


def assemble(local, upper, lower, place):
    edge = jnp.concatenate([upper, lower], axis=0)
    return (local.astype(F32) + dot(place, edge)).astype(BF16)


def make_step_kernel(hop, first, count, fresh):
    def body(hop_ref, *refs):
        inputs, refs = (refs[:1], refs[1:]) if hop == 0 else (refs[:4], refs[4:])
        slope_ref, own_ref, halo_ref, w1_ref, w2_ref = refs[:5]
        refs = refs[5:] if fresh else refs[10:]
        sent, kept, (g_buf, dz_buf, sems) = refs[:3], refs[3:8], refs[8:]

        @pl.when(hop_ref[0] == hop)
        def _():
            if hop == 0:
                g = [inputs[0][first + j] for j in range(count)]
            else:
                loc_ref, upper_ref, lower_ref, place_ref = inputs
                g = [assemble(loc_ref[j], upper_ref[j], lower_ref[j], place_ref[...]) for j in range(count)]
            layer_step(g, first, slope_ref, own_ref, halo_ref, w1_ref, w2_ref, sent, kept, g_buf, dz_buf, sems)

    return body


def weight_kernel(x_ref, agg_ref, act_ref, g_ref, dz_ref, grad_ref):
    batches, rows, width = x_ref.shape
    total = batches * rows
    g = g_ref[...].reshape(total, width)
    dz = dz_ref[...].reshape(total, width)
    over = ((0,), (0,))
    grad_ref[:width] = dot(x_ref[...].reshape(total, width), dz, over)
    grad_ref[width : 2 * width] = dot(agg_ref[...].reshape(total, width), dz, over)
    grad_ref[2 * width :] = dot(act_ref[...].reshape(total, width), g, over)


def finish_kernel(loc_ref, upper_ref, lower_ref, place_ref, out_ref):
    for m in range(loc_ref.shape[0]):
        out_ref[m] = assemble(loc_ref[m], upper_ref[m], lower_ref[m], place_ref[...])


def sum_over_dom(part, count):
    if count & (count - 1) or count < 4:
        return lax.psum(part, "dom")
    me = lax.axis_index("dom")

    def swap(value, mask):
        return lax.ppermute(value, "dom", [(i, i ^ mask) for i in range(count)])

    half = part.shape[0] // 2
    low = me % 2 == 0
    keep = jnp.where(low, part[:half], part[half:])
    give = jnp.where(low, part[half:], part[:half]).astype(BF16)
    acc = keep + swap(give, 1).astype(F32)
    bit = 2
    while bit < count:
        mine = acc.astype(BF16)
        if bit * 2 < count:
            others = [swap(mine, mask) for mask in (bit, 2 * bit, 3 * bit)]
            a, b, c = [other.astype(F32) for other in others]
            acc = (mine.astype(F32) + a) + (b + c)
            bit *= 4
        else:
            acc = mine.astype(F32) + swap(mine, bit).astype(F32)
            bit *= 2
    mine = acc.astype(BF16)
    other = swap(mine, 1)
    first = jnp.where(low, mine, other)
    second = jnp.where(low, other, mine)
    return jnp.concatenate([first, second], axis=0).astype(F32)


def per_device(saved_inputs, grad_out, w_first, w_second, face_weight, neighbours, send_rows):
    x = saved_inputs[0]
    w1 = w_first[0]
    w2 = w_second[0]
    batches, rows, width = x.shape
    slots = send_rows.shape[1]
    sections = lax.axis_size("section")
    doms = lax.axis_size("dom")
    chunks = CHUNKS if batches % CHUNKS == 0 else 1
    count = batches // chunks
    hop_here = (sections - 1 - lax.axis_index("section")).astype(jnp.int32).reshape(1)
    sds = jax.ShapeDtypeStruct

    place, up, down = pl.pallas_call(
        pack_kernel,
        out_shape=(sds((rows, 2 * slots), BF16), sds((batches, slots, width), BF16),
                   sds((batches, slots, width), BF16)),
        compiler_params=params(), name="pack",
    )(x, send_rows)
    rise = [(i, i + 1) for i in range(doms - 1)]
    fall = [(i + 1, i) for i in range(doms - 1)]
    below = lax.ppermute(up, "dom", rise)
    above = lax.ppermute(down, "dom", fall)

    slope, act, agg, own, halo = pl.pallas_call(
        forward_kernel,
        out_shape=(sds((batches, rows, width), F32), sds((batches, rows, width), BF16),
                   sds((batches, rows, width), BF16), sds((rows, rows), BF16), sds((2 * slots, rows), BF16)),
        compiler_params=params(), name="forward",
    )(x, below, above, neighbours, face_weight, w1)

    def move(value, hop, shift):
        source = sections - 1 - hop
        pairs = [(p * sections + source, (p + shift) * sections + source - 1)
                 for p in range(doms) if 0 <= p + shift < doms]
        return lax.ppermute(value, ("dom", "section"), pairs)

    def shapes(n):
        full, edge = sds((n, rows, width), BF16), sds((n, slots, width), BF16)
        return (full, edge, edge)

    any_spec = pl.BlockSpec(memory_space=pl.ANY)
    kept = ()
    received = [None] * chunks
    for hop in range(sections):
        sent = []
        for c in range(chunks):
            inputs = (grad_out,) if hop == 0 else (*received[c], place)
            inputs = (hop_here, *inputs, slope, own, halo, w1, w2)
            outs = pl.pallas_call(
                make_step_kernel(hop, c * count, count, not kept),
                in_specs=[pl.BlockSpec(memory_space=pltpu.SMEM)] + [vmem()] * (len(inputs) - 1)
                + [any_spec] * len(kept),
                out_specs=[vmem()] * 3 + [any_spec] * 5,
                out_shape=shapes(count) + shapes(batches) + (shapes(batches)[0],) * 2,
                scratch_shapes=[pltpu.VMEM((count, rows, width), BF16), pltpu.VMEM((count, rows, width), BF16),
                                pltpu.SemaphoreType.DMA((5,))],
                input_output_aliases={len(inputs) + n: 3 + n for n in range(len(kept))},
                cost_estimate=pl.CostEstimate(flops=STEP_FLOPS, bytes_accessed=1 << 20, transcendentals=0),
                compiler_params=params(), name="step",
            )(*inputs, *kept)
            kept = outs[3:]
            if hop + 1 < sections:
                local, to_below, to_above = outs[:3]
                sent.append((move(local, hop, 0), move(to_below, hop, -1), move(to_above, hop, 1)))
        received = sent
    local, to_below, to_above, g, dz = kept

    grad = pl.pallas_call(
        weight_kernel, out_shape=sds((3 * width, width), F32),
        compiler_params=params(), name="weights",
    )(x, agg, act, g, dz)

    total = sum_over_dom(grad, doms)
    from_upper = lax.ppermute(to_below, "dom", fall)
    from_lower = lax.ppermute(to_above, "dom", rise)
    grad_in = pl.pallas_call(
        finish_kernel, out_shape=sds((batches, rows, width), BF16),
        compiler_params=params(), name="finish",
    )(local, from_upper, from_lower, place)
    return grad_in[None], total[None, : 2 * width], total[None, 2 * width :]


def solution(mesh):
    return jax.shard_map(
        per_device,
        mesh=mesh,
        in_specs=(
            P("section", None, "dom", None),
            P(None, "dom", None),
            P("section", None, None),
            P("section", None, None),
            P(None, "dom"),
            P(None, "dom"),
            P(None, "dom"),
        ),
        out_specs=(
            P("section", None, "dom", None),
            P("section", None, None),
            P("section", None, None),
        ),
        check_vma=False,
    )
```

```python
import jax
import jax.numpy as jnp
from jax import lax
from jax.experimental import pallas as pl
from jax.experimental.pallas import tpu as pltpu
from jax.sharding import PartitionSpec as P

F32 = jnp.float32
BF16 = jnp.bfloat16
CHUNKS = 2
STEP_FLOPS = 10**11


def dot(a, b, dims=((1,), (0,))):
    return lax.dot_general(a, b, (dims, ((), ())), preferred_element_type=F32)


def vmem():
    return pl.BlockSpec(memory_space=pltpu.VMEM)


def params():
    return pltpu.CompilerParams(vmem_limit_bytes=16 * 1024 * 1024)


def load_kernel(odd_ref, x_hbm, g_hbm, w1_hbm, w2_hbm, nbr_hbm, coef_hbm, send_hbm,
                x_ref, g_ref, w1_ref, w2_ref, nbr_ref, coef_ref, place_ref, near_ref, far_ref, send_ref, sems):
    sources = (send_hbm, x_hbm, nbr_hbm, coef_hbm, w1_hbm, w2_hbm, g_hbm)
    targets = (send_ref, x_ref, nbr_ref, coef_ref, w1_ref, w2_ref, g_ref)
    copies = [pltpu.make_async_copy(source, target, sems.at[n])
              for n, (source, target) in enumerate(zip(sources, targets))]
    for copy in copies:
        copy.start()
    batches, rows, _ = x_ref.shape
    slots = send_ref.shape[1]
    row = lax.broadcasted_iota(jnp.int32, (rows, slots), 0)
    copies[0].wait()
    up = jnp.where(row == send_ref[0:1, :], 1.0, 0.0)
    down = jnp.where(row == send_ref[1:2, :], 1.0, 0.0)
    place = jnp.concatenate([up, down], axis=1)
    place_ref[...] = place.astype(BF16)
    pick = place.T.astype(BF16)
    copies[1].wait()
    odd = odd_ref[0] == 1
    for m in range(batches):
        sent = dot(pick, x_ref[m])
        up, down = sent[:slots], sent[slots:]
        near_ref[m] = jnp.where(odd, down, up).astype(BF16)
        far_ref[m] = jnp.where(odd, up, down).astype(BF16)
    for copy in copies[2:]:
        copy.wait()


def forward_kernel(odd_ref, x_ref, near_ref, far_ref, nbr_ref, coef_ref, w_ref,
                   slope_ref, act_ref, agg_ref, own_ref, halo_ref):
    batches, rows, width = x_ref.shape
    slots = near_ref.shape[1]
    faces = nbr_ref.shape[0]
    slot = lax.broadcasted_iota(jnp.int32, (rows + 2 * slots, rows), 0)
    spread = jnp.zeros((rows + 2 * slots, rows), F32)
    for k in range(faces):
        spread = spread + jnp.where(slot == nbr_ref[k : k + 1, :], coef_ref[k : k + 1, :], 0.0)
    own = spread[slots : slots + rows]
    lower, upper = spread[:slots], spread[slots + rows :]
    halo_ref[...] = jnp.concatenate([lower, upper], axis=0).astype(BF16)
    own_ref[...] = own.astype(BF16)
    own_t = own.T.astype(BF16)
    odd = odd_ref[0] == 1
    near = jnp.where(odd, lower, upper)
    far = jnp.where(odd, upper, lower)
    halo_t = jnp.concatenate([near, far], axis=0).T.astype(BF16)
    for m in range(batches):
        x = x_ref[m]
        edge = jnp.concatenate([near_ref[m], far_ref[m]], axis=0)
        agg = (dot(own_t, x) + dot(halo_t, edge)).astype(BF16)
        z = dot(x, w_ref[:width]) + dot(agg, w_ref[width:])
        sig = 1.0 / (1.0 + jnp.exp(-z))
        agg_ref[m] = agg
        act_ref[m] = (z * sig).astype(BF16)
        slope_ref[m] = sig * (1.0 + z * (1.0 - sig))


def layer_step(g, first, slope_ref, own_ref, halo_ref, w1_ref, w2_ref, sent, kept, g_buf, dz_buf, sems):
    rows, width = slope_ref.shape[1], slope_ref.shape[2]
    local_ref, below_ref, above_ref = sent
    slots = below_ref.shape[1]
    count = len(g)
    copies = []

    def keep(n, source):
        copy = pltpu.make_async_copy(source, kept[n].at[pl.ds(first, count)], sems.at[n])
        copy.start()
        copies.append(copy)

    for j in range(count):
        g_buf[j] = g[j]
    keep(3, g_buf)
    stacked = jnp.concatenate(g, axis=0) if count > 1 else g[0]
    d_act = dot(stacked, w2_ref[...], ((1,), (1,)))
    dzs = []
    for j in range(count):
        dz = (d_act[j * rows : (j + 1) * rows] * slope_ref[first + j]).astype(BF16)
        dz_buf[j] = dz
        dzs.append(dz)
    keep(4, dz_buf)
    dz = jnp.concatenate(dzs, axis=0) if count > 1 else dzs[0]
    dj = dot(dz, w1_ref[...], ((1,), (1,)))
    for j in range(count):
        part = dj[j * rows : (j + 1) * rows]
        dagg = part[:, width:].astype(BF16)
        local = g[j].astype(F32) + part[:, :width] + dot(own_ref[...], dagg)
        local_ref[j] = local.astype(BF16)
        edge = dot(halo_ref[...], dagg).astype(BF16)
        below_ref[j] = edge[:slots]
        above_ref[j] = edge[slots:]
    for n in range(3):
        keep(n, sent[n])
    for copy in copies:
        copy.wait()


def assemble(local, upper, lower, place):
    edge = jnp.concatenate([upper, lower], axis=0)
    return (local.astype(F32) + dot(place, edge)).astype(BF16)


def make_step_kernel(hop, first, count, fresh):
    def body(hop_ref, *refs):
        inputs, refs = (refs[:1], refs[1:]) if hop == 0 else (refs[:4], refs[4:])
        slope_ref, own_ref, halo_ref, w1_ref, w2_ref = refs[:5]
        refs = refs[5:] if fresh else refs[10:]
        sent, kept, (g_buf, dz_buf, sems) = refs[:3], refs[3:8], refs[8:]

        @pl.when(hop_ref[0] == hop)
        def _():
            if hop == 0:
                g = [inputs[0][first + j] for j in range(count)]
            else:
                loc_ref, upper_ref, lower_ref, place_ref = inputs
                g = [assemble(loc_ref[j], upper_ref[j], lower_ref[j], place_ref[...]) for j in range(count)]
            layer_step(g, first, slope_ref, own_ref, halo_ref, w1_ref, w2_ref, sent, kept, g_buf, dz_buf, sems)

    return body


def weight_kernel(odd_ref, x_ref, agg_ref, act_ref, g_ref, dz_ref, to_below_ref, to_above_ref,
                  keep_ref, give_ref, near_ref, far_ref, grad_ref):
    batches, rows, width = x_ref.shape
    total = batches * rows
    g = g_ref[...].reshape(total, width)
    dz = dz_ref[...].reshape(total, width)
    over = ((0,), (0,))
    grad_ref[:width] = dot(x_ref[...].reshape(total, width), dz, over)
    grad_ref[width : 2 * width] = dot(agg_ref[...].reshape(total, width), dz, over)
    grad_ref[2 * width :] = dot(act_ref[...].reshape(total, width), g, over)
    half = keep_ref.shape[0]
    odd = odd_ref[0]
    keep_ref[...] = grad_ref[pl.ds(pl.multiple_of(odd * half, half), half)]
    give_ref[...] = grad_ref[pl.ds(pl.multiple_of((1 - odd) * half, half), half)].astype(BF16)
    below, above = to_below_ref[...], to_above_ref[...]
    near_ref[...] = jnp.where(odd == 1, below, above)
    far_ref[...] = jnp.where(odd == 1, above, below)


def total_kernel(*refs):
    parts, out_ref = refs[:-3], refs[-1]
    values = [part[...].astype(F32) for part in parts]
    while len(values) > 1:
        values = [values[n] + values[n + 1] for n in range(0, len(values), 2)]
    out_ref[...] = values[0].astype(BF16)


def split_kernel(odd_ref, mine_ref, other_ref, first_ref, second_ref):
    half = mine_ref.shape[0]
    size = first_ref.shape[0]
    odd = odd_ref[0] == 1
    mine, other = mine_ref[...].astype(F32), other_ref[...].astype(F32)
    low = jnp.where(odd, other, mine)
    high = jnp.where(odd, mine, other)
    first_ref[:half] = low
    first_ref[half:] = high[: size - half]
    second_ref[...] = high[size - half :]


def finish_kernel(odd_ref, loc_ref, near_ref, far_ref, place_ref, out_ref):
    odd = odd_ref[0] == 1
    for m in range(loc_ref.shape[0]):
        near, far = near_ref[m], far_ref[m]
        upper = jnp.where(odd, far, near)
        lower = jnp.where(odd, near, far)
        out_ref[m] = assemble(loc_ref[m], upper, lower, place_ref[...])


def per_device(saved_inputs, grad_out, w_first, w_second, face_weight, neighbours, send_rows):
    x = saved_inputs[0]
    w1 = w_first[0]
    w2 = w_second[0]
    batches, rows, width = x.shape
    slots = send_rows.shape[1]
    sections = lax.axis_size("section")
    doms = lax.axis_size("dom")
    chunks = CHUNKS if batches % CHUNKS == 0 else 1
    count = batches // chunks
    hop_here = (sections - 1 - lax.axis_index("section")).astype(jnp.int32).reshape(1)
    odd = (lax.axis_index("dom") % 2).astype(jnp.int32).reshape(1)
    sds = jax.ShapeDtypeStruct
    smem = pl.BlockSpec(memory_space=pltpu.SMEM)
    any_spec = pl.BlockSpec(memory_space=pl.ANY)
    hbm_spec = pl.BlockSpec(memory_space=pltpu.HBM)

    def like(value):
        return sds(value.shape, value.dtype)

    def call(body, outs, *args, scratch=(), name):
        return pl.pallas_call(
            body, in_specs=[smem] + [vmem()] * (len(args) - 1), out_specs=[vmem()] * len(outs), out_shape=outs,
            scratch_shapes=scratch, compiler_params=params(), name=name,
        )(*args)

    near_pairs = [(p, p ^ 1) for p in range(doms)]
    far_pairs = [(p, p + 1 if p % 2 else p - 1) for p in range(1, doms - 1)]

    def exchange(near, far):
        return lax.ppermute(near, "dom", near_pairs), lax.ppermute(far, "dom", far_pairs)

    edge_shape = sds((batches, slots, width), BF16)
    x, grad_out, w1, w2, neighbours, face_weight, place, near, far = pl.pallas_call(
        load_kernel,
        in_specs=[smem] + [hbm_spec] * 7,
        out_specs=[vmem()] * 9,
        out_shape=(like(x), like(grad_out), like(w1), like(w2), like(neighbours), like(face_weight),
                   sds((rows, 2 * slots), BF16), edge_shape, edge_shape),
        scratch_shapes=[pltpu.VMEM(send_rows.shape, send_rows.dtype), pltpu.SemaphoreType.DMA((7,))],
        compiler_params=params(), name="load",
    )(odd, *[pltpu.with_memory_space_constraint(value, pltpu.HBM)
             for value in (x, grad_out, w1, w2, neighbours, face_weight, send_rows)])
    near, far = exchange(near, far)

    full_shape = sds((batches, rows, width), BF16)
    slope, act, agg, own, halo = call(
        forward_kernel,
        (sds((batches, rows, width), F32), full_shape, full_shape, sds((rows, rows), BF16),
         sds((2 * slots, rows), BF16)),
        odd, x, near, far, neighbours, face_weight, w1, name="forward")

    def move(value, hop, shift):
        source = sections - 1 - hop
        pairs = [(p * sections + source, (p + shift) * sections + source - 1)
                 for p in range(doms) if 0 <= p + shift < doms]
        return lax.ppermute(value, ("dom", "section"), pairs)

    def shapes(n):
        full, edge = sds((n, rows, width), BF16), sds((n, slots, width), BF16)
        return (full, edge, edge)

    kept = ()
    received = [None] * chunks
    for hop in range(sections):
        sent = []
        for c in range(chunks):
            inputs = (grad_out,) if hop == 0 else (*received[c], place)
            inputs = (hop_here, *inputs, slope, own, halo, w1, w2)
            outs = pl.pallas_call(
                make_step_kernel(hop, c * count, count, not kept),
                in_specs=[pl.BlockSpec(memory_space=pltpu.SMEM)] + [vmem()] * (len(inputs) - 1)
                + [any_spec] * len(kept),
                out_specs=[vmem()] * 3 + [any_spec] * 5,
                out_shape=shapes(count) + shapes(batches) + (shapes(batches)[0],) * 2,
                scratch_shapes=[pltpu.VMEM((count, rows, width), BF16), pltpu.VMEM((count, rows, width), BF16),
                                pltpu.SemaphoreType.DMA((5,))],
                input_output_aliases={len(inputs) + n: 3 + n for n in range(len(kept))},
                cost_estimate=pl.CostEstimate(flops=STEP_FLOPS, bytes_accessed=1 << 20, transcendentals=0),
                compiler_params=params(), name="step",
            )(*inputs, *kept)
            kept = outs[3:]
            if hop + 1 < sections:
                local, to_below, to_above = outs[:3]
                sent.append((move(local, hop, 0), move(to_below, hop, -1), move(to_above, hop, 1)))
        received = sent
    local, to_below, to_above, g, dz = kept

    half = sds((3 * width // 2, width), BF16)
    keep, give, near, far = call(
        weight_kernel, (sds(half.shape, F32), half, edge_shape, edge_shape),
        odd, x, agg, act, g, dz, to_below, to_above,
        scratch=[pltpu.VMEM((3 * width, width), F32)], name="weights")

    def swap(value, mask):
        return lax.ppermute(value, "dom", [(i, i ^ mask) for i in range(doms)])

    mine = (keep + swap(give, 1).astype(F32)).astype(BF16)
    near, far = exchange(near, far)
    bit = 2
    while bit < doms:
        masks = (bit, 2 * bit, 3 * bit) if bit * 2 < doms else (bit,)
        parts = [mine] + [swap(mine, mask) for mask in masks]
        mine = pl.pallas_call(
            total_kernel, in_specs=[vmem()] * len(parts) + [any_spec] * 2, out_specs=vmem(), out_shape=half,
            compiler_params=params(), name="total",
        )(*parts, near, far)
        bit *= len(parts)
    other = swap(mine, 1)
    (grad_in,) = call(finish_kernel, (full_shape,), odd, local, near, far, place, name="finish")
    first, second = call(
        split_kernel, (sds((2 * width, width), F32), sds((width, width), F32)), odd, mine, other, name="split")
    return grad_in[None], first[None], second[None]


def solution(mesh):
    return jax.shard_map(
        per_device,
        mesh=mesh,
        in_specs=(
            P("section", None, "dom", None),
            P(None, "dom", None),
            P("section", None, None),
            P("section", None, None),
            P(None, "dom"),
            P(None, "dom"),
            P(None, "dom"),
        ),
        out_specs=(
            P("section", None, "dom", None),
            P("section", None, None),
            P("section", None, None),
        ),
        check_vma=False,
    )
```

```python
import jax
import jax.numpy as jnp
from jax import lax
from jax.experimental import pallas as pl
from jax.experimental.pallas import tpu as pltpu
from jax.sharding import PartitionSpec as P

F32 = jnp.float32
BF16 = jnp.bfloat16
CHUNKS = 2
STEP_FLOPS = 2700 * 10**6
LAST_FLOPS = 2754 * 10**6


def dot(a, b, dims=((1,), (0,))):
    return lax.dot_general(a, b, (dims, ((), ())), preferred_element_type=F32)


def vmem():
    return pl.BlockSpec(memory_space=pltpu.VMEM)


def params():
    return pltpu.CompilerParams(vmem_limit_bytes=16 * 1024 * 1024)


def load_kernel(odd_ref, x_hbm, g_hbm, w1_hbm, w2_hbm, nbr_hbm, coef_hbm, send_hbm,
                x_ref, g_ref, w1_ref, w2_ref, nbr_ref, coef_ref, place_ref, near_ref, far_ref, send_ref, sems):
    sources = (send_hbm, x_hbm, nbr_hbm, coef_hbm, w1_hbm, w2_hbm, g_hbm)
    targets = (send_ref, x_ref, nbr_ref, coef_ref, w1_ref, w2_ref, g_ref)
    copies = [pltpu.make_async_copy(source, target, sems.at[n])
              for n, (source, target) in enumerate(zip(sources, targets))]
    for copy in copies:
        copy.start()
    batches, rows, _ = x_ref.shape
    slots = send_ref.shape[1]
    row = lax.broadcasted_iota(jnp.int32, (rows, slots), 0)
    copies[0].wait()
    up = jnp.where(row == send_ref[0:1, :], 1.0, 0.0)
    down = jnp.where(row == send_ref[1:2, :], 1.0, 0.0)
    place = jnp.concatenate([up, down], axis=1)
    place_ref[...] = place.astype(BF16)
    pick = place.T.astype(BF16)
    copies[1].wait()
    odd = odd_ref[0] == 1
    for m in range(batches):
        sent = dot(pick, x_ref[m])
        up, down = sent[:slots], sent[slots:]
        near_ref[m] = jnp.where(odd, down, up).astype(BF16)
        far_ref[m] = jnp.where(odd, up, down).astype(BF16)
    for copy in copies[2:]:
        copy.wait()


def forward_kernel(odd_ref, x_ref, near_ref, far_ref, nbr_ref, coef_ref, w_ref,
                   slope_ref, act_ref, agg_ref, own_ref, halo_ref):
    batches, rows, width = x_ref.shape
    slots = near_ref.shape[1]
    faces = nbr_ref.shape[0]
    slot = lax.broadcasted_iota(jnp.int32, (rows + 2 * slots, rows), 0)
    spread = jnp.zeros((rows + 2 * slots, rows), F32)
    for k in range(faces):
        spread = spread + jnp.where(slot == nbr_ref[k : k + 1, :], coef_ref[k : k + 1, :], 0.0)
    own = spread[slots : slots + rows]
    lower, upper = spread[:slots], spread[slots + rows :]
    halo_ref[...] = jnp.concatenate([lower, upper], axis=0).astype(BF16)
    own_ref[...] = own.astype(BF16)
    own_t = own.T.astype(BF16)
    odd = odd_ref[0] == 1
    near = jnp.where(odd, lower, upper)
    far = jnp.where(odd, upper, lower)
    halo_t = jnp.concatenate([near, far], axis=0).T.astype(BF16)
    for m in range(batches):
        x = x_ref[m]
        edge = jnp.concatenate([near_ref[m], far_ref[m]], axis=0)
        agg = (dot(own_t, x) + dot(halo_t, edge)).astype(BF16)
        z = dot(x, w_ref[:width]) + dot(agg, w_ref[width:])
        sig = 1.0 / (1.0 + jnp.exp(-z))
        agg_ref[m] = agg
        act_ref[m] = (z * sig).astype(BF16)
        slope_ref[m] = sig * (1.0 + z * (1.0 - sig))


def layer_step(g, first, slope_ref, own_ref, halo_ref, w1_ref, w2_ref, sent, kept, g_buf, dz_buf, sems):
    rows, width = slope_ref.shape[1], slope_ref.shape[2]
    local_ref, below_ref, above_ref = sent
    slots = below_ref.shape[1]
    count = len(g)
    copies = []

    def keep(n, source, j):
        copy = pltpu.make_async_copy(source.at[j], kept[n].at[first + j], sems.at[n, j])
        copy.start()
        copies.append(copy)

    for j in range(count):
        g_buf[j] = g[j]
        keep(3, g_buf, j)
    stacked = jnp.concatenate(g, axis=0) if count > 1 else g[0]
    d_act = dot(stacked, w2_ref[...], ((1,), (1,)))
    dzs = []
    for j in range(count):
        dz = (d_act[j * rows : (j + 1) * rows] * slope_ref[first + j]).astype(BF16)
        dz_buf[j] = dz
        keep(4, dz_buf, j)
        dzs.append(dz)
    dz = jnp.concatenate(dzs, axis=0) if count > 1 else dzs[0]
    dj = dot(dz, w1_ref[...], ((1,), (1,)))
    for j in range(count):
        part = dj[j * rows : (j + 1) * rows]
        dagg = part[:, width:].astype(BF16)
        local = g[j].astype(F32) + part[:, :width] + dot(own_ref[...], dagg)
        local_ref[j] = local.astype(BF16)
        keep(0, local_ref, j)
        edge = dot(halo_ref[...], dagg).astype(BF16)
        below_ref[j] = edge[:slots]
        above_ref[j] = edge[slots:]
        keep(1, below_ref, j)
        keep(2, above_ref, j)
    for copy in copies:
        copy.wait()


def assemble(local, upper, lower, place):
    edge = jnp.concatenate([upper, lower], axis=0)
    return (local.astype(F32) + dot(place, edge)).astype(BF16)


def make_step_kernel(hop, first, count, fresh, last):
    def body(hop_ref, *refs):
        inputs, refs = (refs[:1], refs[1:]) if hop == 0 else (refs[:4], refs[4:])
        slope_ref, own_ref, halo_ref, w1_ref, w2_ref = refs[:5]
        refs = refs[5:] if fresh else refs[10:]
        if last:
            kept, g_buf, dz_buf, sems, *sent = refs[:5], *refs[5:]
        else:
            sent, kept, (g_buf, dz_buf, sems) = refs[:3], refs[3:8], refs[8:]

        @pl.when(hop_ref[0] == hop)
        def _():
            if hop == 0:
                g = [inputs[0][first + j] for j in range(count)]
            else:
                loc_ref, upper_ref, lower_ref, place_ref = inputs
                g = [assemble(loc_ref[j], upper_ref[j], lower_ref[j], place_ref[...]) for j in range(count)]
            layer_step(g, first, slope_ref, own_ref, halo_ref, w1_ref, w2_ref, sent, kept, g_buf, dz_buf, sems)

    return body


def weight_kernel(odd_ref, x_ref, agg_ref, act_ref, g_ref, dz_ref, to_below_ref, to_above_ref,
                  keep_ref, give_ref, far_ref, grad_ref):
    batches, rows, width = x_ref.shape
    total = batches * rows
    g = g_ref[...].reshape(total, width)
    dz = dz_ref[...].reshape(total, width)
    over = ((0,), (0,))
    grad_ref[:width] = dot(x_ref[...].reshape(total, width), dz, over)
    grad_ref[width : 2 * width] = dot(agg_ref[...].reshape(total, width), dz, over)
    grad_ref[2 * width :] = dot(act_ref[...].reshape(total, width), g, over)
    half = keep_ref.shape[0]
    odd = odd_ref[0]
    keep_ref[...] = grad_ref[pl.ds(pl.multiple_of(odd * half, half), half)]
    give_ref[:half] = grad_ref[pl.ds(pl.multiple_of((1 - odd) * half, half), half)].astype(BF16)
    below, above = to_below_ref[...], to_above_ref[...]
    give_ref[half:] = jnp.where(odd == 1, below, above).reshape(give_ref.shape[0] - half, width)
    far_ref[...] = jnp.where(odd == 1, above, below)


def add(a, b):
    return (a.astype(F32) + b.astype(F32)).astype(BF16)


def join_kernel(p_ref, p_other_ref, q_ref, q_other_ref, far_ref, out_ref):
    quarter = p_ref.shape[0]
    out_ref[:quarter] = add(p_ref[...], p_other_ref[...])
    out_ref[quarter:] = add(q_ref[...], q_other_ref[...])


def split_kernel(odd_ref, mine_ref, other_ref, first_ref, second_ref):
    half = mine_ref.shape[0]
    size = first_ref.shape[0]
    odd = odd_ref[0] == 1
    mine, other = mine_ref[...].astype(F32), other_ref[...].astype(F32)
    low = jnp.where(odd, other, mine)
    high = jnp.where(odd, mine, other)
    first_ref[:half] = low
    first_ref[half:] = high[: size - half]
    second_ref[...] = high[size - half :]


def finish_kernel(odd_ref, loc_ref, came_ref, far_ref, place_ref, out_ref):
    odd = odd_ref[0] == 1
    batches, slots = far_ref.shape[:2]
    start = came_ref.shape[0] - batches * slots
    for m in range(batches):
        near, far = came_ref[start + m * slots : start + (m + 1) * slots], far_ref[m]
        upper = jnp.where(odd, far, near)
        lower = jnp.where(odd, near, far)
        out_ref[m] = assemble(loc_ref[m], upper, lower, place_ref[...])


def per_device(saved_inputs, grad_out, w_first, w_second, face_weight, neighbours, send_rows):
    x = saved_inputs[0]
    w1 = w_first[0]
    w2 = w_second[0]
    batches, rows, width = x.shape
    slots = send_rows.shape[1]
    sections = lax.axis_size("section")
    doms = lax.axis_size("dom")
    chunks = CHUNKS if batches % CHUNKS == 0 else 1
    count = batches // chunks
    hop_here = (sections - 1 - lax.axis_index("section")).astype(jnp.int32).reshape(1)
    odd = (lax.axis_index("dom") % 2).astype(jnp.int32).reshape(1)
    sds = jax.ShapeDtypeStruct
    smem = pl.BlockSpec(memory_space=pltpu.SMEM)
    any_spec = pl.BlockSpec(memory_space=pl.ANY)
    hbm_spec = pl.BlockSpec(memory_space=pltpu.HBM)

    def like(value):
        return sds(value.shape, value.dtype)

    def call(body, outs, *args, scratch=(), name):
        return pl.pallas_call(
            body, in_specs=[smem] + [vmem()] * (len(args) - 1), out_specs=[vmem()] * len(outs), out_shape=outs,
            scratch_shapes=scratch, compiler_params=params(), name=name,
        )(*args)

    near_pairs = [(p, p ^ 1) for p in range(doms)]
    far_pairs = [(p, p + 1 if p % 2 else p - 1) for p in range(1, doms - 1)]

    def exchange(near, far):
        return lax.ppermute(near, "dom", near_pairs), lax.ppermute(far, "dom", far_pairs)

    edge_shape = sds((batches, slots, width), BF16)
    x, grad_out, w1, w2, neighbours, face_weight, place, near, far = pl.pallas_call(
        load_kernel,
        in_specs=[smem] + [hbm_spec] * 7,
        out_specs=[vmem()] * 9,
        out_shape=(like(x), like(grad_out), like(w1), like(w2), like(neighbours), like(face_weight),
                   sds((rows, 2 * slots), BF16), edge_shape, edge_shape),
        scratch_shapes=[pltpu.VMEM(send_rows.shape, send_rows.dtype), pltpu.SemaphoreType.DMA((7,))],
        compiler_params=params(), name="load",
    )(odd, *[pltpu.with_memory_space_constraint(value, pltpu.HBM)
             for value in (x, grad_out, w1, w2, neighbours, face_weight, send_rows)])
    near, far = exchange(near, far)

    full_shape = sds((batches, rows, width), BF16)
    slope, act, agg, own, halo = call(
        forward_kernel,
        (sds((batches, rows, width), F32), full_shape, full_shape, sds((rows, rows), BF16),
         sds((2 * slots, rows), BF16)),
        odd, x, near, far, neighbours, face_weight, w1, name="forward")

    def move(value, hop, shift):
        source = sections - 1 - hop
        pairs = [(p * sections + source, (p + shift) * sections + source - 1)
                 for p in range(doms) if 0 <= p + shift < doms]
        return lax.ppermute(value, ("dom", "section"), pairs)

    def shapes(n):
        full, edge = sds((n, rows, width), BF16), sds((n, slots, width), BF16)
        return (full, edge, edge)

    kept = ()
    received = [None] * chunks
    for hop in range(sections):
        sent = []
        for c in range(chunks):
            inputs = (grad_out,) if hop == 0 else (*received[c], place)
            inputs = (hop_here, *inputs, slope, own, halo, w1, w2)
            last = hop + 1 == sections
            sends = () if last else shapes(count)
            buffers = [pltpu.VMEM((count, rows, width), BF16)] * 2 + [pltpu.SemaphoreType.DMA((5, count))]
            if last:
                buffers += [pltpu.VMEM(shape.shape, shape.dtype) for shape in shapes(count)]
            outs = pl.pallas_call(
                make_step_kernel(hop, c * count, count, not kept, last),
                in_specs=[smem] + [vmem()] * (len(inputs) - 1) + [any_spec] * len(kept),
                out_specs=[vmem()] * len(sends) + [any_spec] * 5,
                out_shape=sends + shapes(batches) + (shapes(batches)[0],) * 2,
                scratch_shapes=buffers,
                input_output_aliases={len(inputs) + n: len(sends) + n for n in range(len(kept))},
                cost_estimate=pl.CostEstimate(flops=LAST_FLOPS if last else STEP_FLOPS, bytes_accessed=1 << 20, transcendentals=0),
                compiler_params=params(), name="step",
            )(*inputs, *kept)
            kept = outs[len(sends):]
            if not last:
                local, to_below, to_above = outs[:3]
                sent.append((move(local, hop, 0), move(to_below, hop, -1), move(to_above, hop, 1)))
        received = sent
    local, to_below, to_above, g, dz = kept

    half = 3 * width // 2
    keep, give, far = call(
        weight_kernel,
        (sds((half, width), F32), sds((half + batches * slots, width), BF16), edge_shape),
        odd, x, agg, act, g, dz, to_below, to_above,
        scratch=[pltpu.VMEM((3 * width, width), F32)], name="weights")

    def swap(value, mask):
        return lax.ppermute(value, "dom", [(i, i ^ mask) for i in range(doms)])

    came = swap(give, 1)
    far = lax.ppermute(far, "dom", far_pairs)
    p = add(keep[: half // 2], came[: half // 2])
    q = add(keep[half // 2 :], came[half // 2 : half])
    bit = 2
    while bit < doms:
        if bit * 2 < doms:
            p, q = add(p, swap(p, bit)), add(q, swap(q, 2 * bit))
            p_other, q_other = swap(p, 2 * bit), swap(q, bit)
        else:
            p_other, q_other = swap(p, bit), swap(q, bit)
        bit *= 4
        if bit < doms:
            p, q = add(p, p_other), add(q, q_other)
    mine = pl.pallas_call(
        join_kernel, in_specs=[vmem()] * 4 + [any_spec], out_specs=vmem(), out_shape=sds((half, width), BF16),
        compiler_params=params(), name="join",
    )(p, p_other, q, q_other, far)
    other = swap(mine, 1)
    (grad_in,) = call(finish_kernel, (full_shape,), odd, local, came, far, place, name="finish")
    first, second = call(
        split_kernel, (sds((2 * width, width), F32), sds((width, width), F32)), odd, mine, other, name="split")
    return grad_in[None], first[None], second[None]


def solution(mesh):
    return jax.shard_map(
        per_device,
        mesh=mesh,
        in_specs=(
            P("section", None, "dom", None),
            P(None, "dom", None),
            P("section", None, None),
            P("section", None, None),
            P(None, "dom"),
            P(None, "dom"),
            P(None, "dom"),
        ),
        out_specs=(
            P("section", None, "dom", None),
            P("section", None, None),
            P("section", None, None),
        ),
        check_vma=False,
    )
```

```python
import jax
import jax.numpy as jnp
from jax import lax
from jax.experimental import pallas as pl
from jax.experimental.pallas import tpu as pltpu
from jax.sharding import PartitionSpec as P

F32 = jnp.float32
BF16 = jnp.bfloat16
CHUNKS = 2
STEP_FLOPS = 10**11


def dot(a, b, dims=((1,), (0,))):
    return lax.dot_general(a, b, (dims, ((), ())), preferred_element_type=F32)


def vmem():
    return pl.BlockSpec(memory_space=pltpu.VMEM)


def params():
    return pltpu.CompilerParams(vmem_limit_bytes=16 * 1024 * 1024)


def load_kernel(odd_ref, x_hbm, g_hbm, w1_hbm, w2_hbm, nbr_hbm, coef_hbm, send_hbm,
                x_ref, g_ref, w1_ref, w2_ref, nbr_ref, coef_ref, place_ref, near_ref, far_ref, send_ref, sems):
    sources = (send_hbm, x_hbm, nbr_hbm, coef_hbm, w1_hbm, w2_hbm, g_hbm)
    targets = (send_ref, x_ref, nbr_ref, coef_ref, w1_ref, w2_ref, g_ref)
    copies = [pltpu.make_async_copy(source, target, sems.at[n])
              for n, (source, target) in enumerate(zip(sources, targets))]
    for copy in copies:
        copy.start()
    batches, rows, _ = x_ref.shape
    slots = send_ref.shape[1]
    row = lax.broadcasted_iota(jnp.int32, (rows, slots), 0)
    copies[0].wait()
    up = jnp.where(row == send_ref[0:1, :], 1.0, 0.0)
    down = jnp.where(row == send_ref[1:2, :], 1.0, 0.0)
    place = jnp.concatenate([up, down], axis=1)
    place_ref[...] = place.astype(BF16)
    pick = place.T.astype(BF16)
    copies[1].wait()
    odd = odd_ref[0] == 1
    for m in range(batches):
        sent = dot(pick, x_ref[m])
        up, down = sent[:slots], sent[slots:]
        near_ref[m] = jnp.where(odd, down, up).astype(BF16)
        far_ref[m] = jnp.where(odd, up, down).astype(BF16)
    for copy in copies[2:]:
        copy.wait()


def inner_kernel(x_ref, nbr_ref, coef_ref, w_ref, base_ref, inner_ref, own_ref, halo_ref):
    batches, rows, width = x_ref.shape
    slots = halo_ref.shape[0] // 2
    faces = nbr_ref.shape[0]
    slot = lax.broadcasted_iota(jnp.int32, (rows + 2 * slots, rows), 0)
    spread = jnp.zeros((rows + 2 * slots, rows), F32)
    for k in range(faces):
        spread = spread + jnp.where(slot == nbr_ref[k : k + 1, :], coef_ref[k : k + 1, :], 0.0)
    own = spread[slots : slots + rows]
    halo_ref[...] = jnp.concatenate([spread[:slots], spread[slots + rows :]], axis=0).astype(BF16)
    own_ref[...] = own.astype(BF16)
    own_t = own.T.astype(BF16)
    for m in range(batches):
        x = x_ref[m]
        inner_ref[m] = dot(own_t, x)
        base_ref[m] = dot(x, w_ref[:width])


def forward_kernel(odd_ref, base_ref, inner_ref, near_ref, far_ref, halo_ref, w_ref, slope_ref, act_ref, agg_ref):
    batches, rows, width = base_ref.shape
    slots = near_ref.shape[1]
    odd = odd_ref[0] == 1
    lower, upper = halo_ref[:slots].astype(F32), halo_ref[slots:].astype(F32)
    near = jnp.where(odd, lower, upper)
    far = jnp.where(odd, upper, lower)
    halo_t = jnp.concatenate([near, far], axis=0).T.astype(BF16)
    for m in range(batches):
        edge = jnp.concatenate([near_ref[m], far_ref[m]], axis=0)
        agg = (inner_ref[m] + dot(halo_t, edge)).astype(BF16)
        z = base_ref[m] + dot(agg, w_ref[width:])
        sig = 1.0 / (1.0 + jnp.exp(-z))
        agg_ref[m] = agg
        act_ref[m] = (z * sig).astype(BF16)
        slope_ref[m] = sig * (1.0 + z * (1.0 - sig))


def assemble(local, upper, lower, place):
    edge = jnp.concatenate([upper, lower], axis=0)
    return (local.astype(F32) + dot(place, edge)).astype(BF16)


def make_step_kernel(hop, first, count):
    def body(hop_ref, *refs):
        *inputs, slope_ref, own_ref, halo_ref, w1_ref, w2_ref, local_ref, below_ref, above_ref, g_ref, dz_ref = refs

        @pl.when(hop_ref[0] == hop)
        def _():
            rows, width = slope_ref.shape[1:]
            slots = below_ref.shape[1]
            if hop == 0:
                g = [inputs[0][first + j] for j in range(count)]
            else:
                loc_ref, upper_ref, lower_ref, place_ref = inputs
                g = [assemble(loc_ref[j], upper_ref[j], lower_ref[j], place_ref[...]) for j in range(count)]
            d_act = dot(jnp.concatenate(g, axis=0), w2_ref[...], ((1,), (1,)))
            dz = [(d_act[j * rows : (j + 1) * rows] * slope_ref[first + j]).astype(BF16) for j in range(count)]
            dj = dot(jnp.concatenate(dz, axis=0), w1_ref[...], ((1,), (1,)))
            for j in range(count):
                part = dj[j * rows : (j + 1) * rows]
                dagg = part[:, width:].astype(BF16)
                local = g[j].astype(F32) + part[:, :width] + dot(own_ref[...], dagg)
                local_ref[j] = local.astype(BF16)
                edge = dot(halo_ref[...], dagg).astype(BF16)
                below_ref[j] = edge[:slots]
                above_ref[j] = edge[slots:]
                g_ref[j] = g[j]
                dz_ref[j] = dz[j]

    return body


def make_weight_kernel(hops, chunks):
    def body(hop_ref, odd_ref, x_ref, agg_ref, act_ref, *refs):
        here = [refs[4 * c : 4 * c + 4] for c in range(chunks)]
        pieces = refs[4 * chunks :]
        local_ref, keep_ref, give_ref, far_ref, grad_ref, below_ref, above_ref, g_ref, dz_ref, sems = refs[-10:]
        targets = (local_ref, below_ref, above_ref, g_ref, dz_ref)
        batches, rows, width = x_ref.shape
        count = batches // chunks

        def copies(hop):
            return [pltpu.make_async_copy(pieces[(hop * chunks + c) * 5 + n],
                                          targets[n].at[pl.ds(c * count, count)], sems.at[n, c])
                    for n in range(5) for c in range(chunks)]

        def gradients(parts):
            over = ((0,), (0,))
            for n, source in enumerate((x_ref, agg_ref, act_ref)):
                total = 0.0
                for first, size, g, dz in parts:
                    left = source[first : first + size].reshape(size * rows, width)
                    right = (g if n == 2 else dz)[...].reshape(size * rows, width)
                    total = total + dot(left, right, over)
                grad_ref[n * width : (n + 1) * width] = total

        for hop in range(hops - 1):
            @pl.when(hop_ref[0] == hop)
            def _():
                for copy in copies(hop):
                    copy.start()

        @pl.when(hop_ref[0] == hops - 1)
        def _():
            gradients([(c * count, count, g, dz) for c, (g, dz, _, _) in enumerate(here)])
            for c, (_, _, below, above) in enumerate(here):
                below_ref[c * count : (c + 1) * count] = below[...]
                above_ref[c * count : (c + 1) * count] = above[...]

        if hops > 1:
            @pl.when(hop_ref[0] != hops - 1)
            def _():
                for copy in copies(0):
                    copy.wait()
                gradients([(0, batches, g_ref, dz_ref)])

        half = keep_ref.shape[0]
        odd = odd_ref[0]
        keep_ref[...] = grad_ref[pl.ds(pl.multiple_of(odd * half, half), half)]
        give_ref[:half] = grad_ref[pl.ds(pl.multiple_of((1 - odd) * half, half), half)].astype(BF16)
        below, above = below_ref[...], above_ref[...]
        give_ref[half:] = jnp.where(odd == 1, below, above).reshape(give_ref.shape[0] - half, width)
        far_ref[...] = jnp.where(odd == 1, above, below)

    return body


def add(a, b):
    return (a.astype(F32) + b.astype(F32)).astype(BF16)


def add_kernel(p_ref, p_other_ref, q_ref, q_other_ref, far_ref, p_out_ref, q_out_ref):
    p_out_ref[...] = add(p_ref[...], p_other_ref[...])
    q_out_ref[...] = add(q_ref[...], q_other_ref[...])


def split_kernel(odd_ref, mine_ref, other_ref, first_ref, second_ref):
    half = mine_ref.shape[0]
    size = first_ref.shape[0]
    odd = odd_ref[0] == 1
    mine, other = mine_ref[...].astype(F32), other_ref[...].astype(F32)
    low = jnp.where(odd, other, mine)
    high = jnp.where(odd, mine, other)
    first_ref[:half] = low
    first_ref[half:] = high[: size - half]
    second_ref[...] = high[size - half :]


def make_finish_kernel(last):
    def body(hop_ref, odd_ref, came_ref, far_ref, place_ref, loc_ref, *refs):
        here, out_ref = refs[:-1], refs[-1]
        odd = odd_ref[0] == 1
        batches, slots = far_ref.shape[:2]
        count = batches // len(here)
        start = came_ref.shape[0] - batches * slots

        def write(local):
            for m in range(batches):
                near, far = came_ref[start + m * slots : start + (m + 1) * slots], far_ref[m]
                upper = jnp.where(odd, far, near)
                lower = jnp.where(odd, near, far)
                out_ref[m] = assemble(local(m), upper, lower, place_ref[...])

        @pl.when(hop_ref[0] == last)
        def _():
            write(lambda m: here[m // count][m % count])

        @pl.when(hop_ref[0] != last)
        def _():
            write(lambda m: loc_ref[m])

    return body


def per_device(saved_inputs, grad_out, w_first, w_second, face_weight, neighbours, send_rows):
    x = saved_inputs[0]
    w1 = w_first[0]
    w2 = w_second[0]
    batches, rows, width = x.shape
    slots = send_rows.shape[1]
    sections = lax.axis_size("section")
    doms = lax.axis_size("dom")
    chunks = CHUNKS if batches % CHUNKS == 0 else 1
    count = batches // chunks
    hop_here = (sections - 1 - lax.axis_index("section")).astype(jnp.int32).reshape(1)
    odd = (lax.axis_index("dom") % 2).astype(jnp.int32).reshape(1)
    sds = jax.ShapeDtypeStruct
    smem = pl.BlockSpec(memory_space=pltpu.SMEM)
    any_spec = pl.BlockSpec(memory_space=pl.ANY)
    hbm_spec = pl.BlockSpec(memory_space=pltpu.HBM)

    def like(value):
        return sds(value.shape, value.dtype)

    def call(body, outs, *args, scratch=(), name):
        return pl.pallas_call(
            body, in_specs=[smem] + [vmem()] * (len(args) - 1), out_specs=[vmem()] * len(outs), out_shape=outs,
            scratch_shapes=scratch, compiler_params=params(), name=name,
        )(*args)

    near_pairs = [(p, p ^ 1) for p in range(doms)]
    far_pairs = [(p, p + 1 if p % 2 else p - 1) for p in range(1, doms - 1)]

    edge_shape = sds((batches, slots, width), BF16)
    x, grad_out, w1, w2, neighbours, face_weight, place, near, far = pl.pallas_call(
        load_kernel,
        in_specs=[smem] + [hbm_spec] * 7,
        out_specs=[vmem()] * 9,
        out_shape=(like(x), like(grad_out), like(w1), like(w2), like(neighbours), like(face_weight),
                   sds((rows, 2 * slots), BF16), edge_shape, edge_shape),
        scratch_shapes=[pltpu.VMEM(send_rows.shape, send_rows.dtype), pltpu.SemaphoreType.DMA((7,))],
        compiler_params=params(), name="load",
    )(odd, *[pltpu.with_memory_space_constraint(value, pltpu.HBM)
             for value in (x, grad_out, w1, w2, neighbours, face_weight, send_rows)])
    near, far = lax.ppermute(near, "dom", near_pairs), lax.ppermute(far, "dom", far_pairs)

    full_shape = sds((batches, rows, width), BF16)
    wide_shape = sds((batches, rows, width), F32)
    base, inner, own, halo = pl.pallas_call(
        inner_kernel, in_specs=[vmem()] * 4, out_specs=[vmem()] * 4,
        out_shape=(wide_shape, wide_shape, sds((rows, rows), BF16), sds((2 * slots, rows), BF16)),
        compiler_params=params(), name="inner",
    )(x, neighbours, face_weight, w1)
    slope, act, agg = call(
        forward_kernel, (wide_shape, full_shape, full_shape), odd, base, inner, near, far, halo, w1, name="forward")

    def move(value, hop, shift):
        source = sections - 1 - hop
        pairs = [(p * sections + source, (p + shift) * sections + source - 1)
                 for p in range(doms) if 0 <= p + shift < doms]
        return lax.ppermute(value, ("dom", "section"), pairs)

    piece, piece_edge = sds((count, rows, width), BF16), sds((count, slots, width), BF16)
    pieces = []
    received = [None] * chunks
    for hop in range(sections):
        sent = []
        for c in range(chunks):
            inputs = (grad_out,) if hop == 0 else (*received[c], place)
            inputs = (hop_here, *inputs, slope, own, halo, w1, w2)
            local, to_below, to_above, g, dz = pl.pallas_call(
                make_step_kernel(hop, c * count, count),
                in_specs=[smem] + [vmem()] * (len(inputs) - 1), out_specs=[vmem()] * 5,
                out_shape=(piece, piece_edge, piece_edge, piece, piece),
                cost_estimate=pl.CostEstimate(flops=STEP_FLOPS, bytes_accessed=1 << 20, transcendentals=0),
                compiler_params=params(), name="step",
            )(*inputs)
            pieces.append((local, to_below, to_above, g, dz))
            if hop + 1 < sections:
                sent.append((move(local, hop, 0), move(to_below, hop, -1), move(to_above, hop, 1)))
        received = sent

    half = 3 * width // 2
    here = [outs[n] for outs in pieces[-chunks:] for n in (3, 4, 1, 2)]
    others = [value for outs in pieces[:-chunks] for value in outs]
    local, keep, give, far = pl.pallas_call(
        make_weight_kernel(sections, chunks),
        in_specs=[smem] * 2 + [vmem()] * (3 + len(here)) + [any_spec] * len(others),
        out_specs=[vmem()] * 4,
        out_shape=(full_shape, sds((half, width), F32), sds((half + batches * slots, width), BF16), edge_shape),
        scratch_shapes=[pltpu.VMEM((3 * width, width), F32), pltpu.VMEM(edge_shape.shape, BF16),
                        pltpu.VMEM(edge_shape.shape, BF16), pltpu.VMEM(full_shape.shape, BF16),
                        pltpu.VMEM(full_shape.shape, BF16), pltpu.SemaphoreType.DMA((5, chunks))],
        compiler_params=params(), name="weights",
    )(hop_here, odd, x, agg, act, *here, *others)

    def swap(value, mask):
        return lax.ppermute(value, "dom", [(i, i ^ mask) for i in range(doms)])

    came = swap(give, 1)
    far = lax.ppermute(far, "dom", far_pairs)
    p = add(keep[: half // 2], came[: half // 2])
    q = add(keep[half // 2 :], came[half // 2 : half])
    bit = 2
    while bit < doms:
        if bit * 2 < doms:
            p, q = pl.pallas_call(
                add_kernel, in_specs=[vmem()] * 4 + [any_spec], out_specs=[vmem()] * 2,
                out_shape=(sds(p.shape, BF16), sds(q.shape, BF16)), compiler_params=params(), name="add",
            )(p, swap(p, bit), q, swap(q, 2 * bit), far)
            p, q = add(p, swap(p, 2 * bit)), add(q, swap(q, bit))
        else:
            p, q = add(p, swap(p, bit)), add(q, swap(q, bit))
        bit *= 4
    mine = jnp.concatenate([p, q], axis=0)
    other = swap(mine, 1)
    grad_in = pl.pallas_call(
        make_finish_kernel(sections - 1), in_specs=[smem] * 2 + [vmem()] * (4 + chunks), out_specs=vmem(),
        out_shape=full_shape, compiler_params=params(), name="finish",
    )(hop_here, odd, came, far, place, local, *[outs[0] for outs in pieces[-chunks:]])
    first, second = call(
        split_kernel, (sds((2 * width, width), F32), sds((width, width), F32)), odd, mine, other, name="split")
    return grad_in[None], first[None], second[None]


def solution(mesh):
    return jax.shard_map(
        per_device,
        mesh=mesh,
        in_specs=(
            P("section", None, "dom", None),
            P(None, "dom", None),
            P("section", None, None),
            P("section", None, None),
            P(None, "dom"),
            P(None, "dom"),
            P(None, "dom"),
        ),
        out_specs=(
            P("section", None, "dom", None),
            P("section", None, None),
            P("section", None, None),
        ),
        check_vma=False,
    )
```

```python
import jax
import jax.numpy as jnp
from jax import lax
from jax.experimental import pallas as pl
from jax.experimental.pallas import tpu as pltpu
from jax.sharding import PartitionSpec as P

F32 = jnp.float32
BF16 = jnp.bfloat16
CHUNKS = 2
STEP_FLOPS = 10**11


def dot(a, b, dims=((1,), (0,))):
    return lax.dot_general(a, b, (dims, ((), ())), preferred_element_type=F32)


def hop_of(info_ref):
    return info_ref[0] >> 2


def odd_of(info_ref):
    return (info_ref[0] >> 1) & 1


def end_of(info_ref):
    return info_ref[0] & 1


def vmem():
    return pl.BlockSpec(memory_space=pltpu.VMEM)


def params():
    return pltpu.CompilerParams(vmem_limit_bytes=16 * 1024 * 1024)


def load_kernel(info_ref, x_hbm, g_hbm, w1_hbm, w2_hbm, nbr_hbm, coef_hbm, send_hbm,
                x_ref, g_ref, w1_ref, w2_ref, nbr_ref, coef_ref, place_ref, near_ref, far_ref, send_ref, sems):
    sources = (send_hbm, x_hbm, nbr_hbm, coef_hbm, w1_hbm, w2_hbm, g_hbm)
    targets = (send_ref, x_ref, nbr_ref, coef_ref, w1_ref, w2_ref, g_ref)
    copies = [pltpu.make_async_copy(source, target, sems.at[n])
              for n, (source, target) in enumerate(zip(sources, targets))]
    for copy in copies:
        copy.start()
    batches, rows, _ = x_ref.shape
    slots = send_ref.shape[1]
    row = lax.broadcasted_iota(jnp.int32, (rows, slots), 0)
    copies[0].wait()
    up = jnp.where(row == send_ref[0:1, :], 1.0, 0.0)
    down = jnp.where(row == send_ref[1:2, :], 1.0, 0.0)
    place = jnp.concatenate([up, down], axis=1)
    place_ref[...] = place.astype(BF16)
    pick = place.T.astype(BF16)
    copies[1].wait()
    odd = odd_of(info_ref) == 1
    for m in range(batches):
        sent = dot(pick, x_ref[m])
        up, down = sent[:slots], sent[slots:]
        near_ref[m] = jnp.where(odd, down, up).astype(BF16)
        far_ref[m] = jnp.where(odd, up, down).astype(BF16)
    for copy in copies[2:]:
        copy.wait()


def inner_kernel(x_ref, nbr_ref, coef_ref, w_ref, base_ref, inner_ref, own_ref, halo_ref):
    batches, rows, width = x_ref.shape
    slots = halo_ref.shape[0] // 2
    faces = nbr_ref.shape[0]
    slot = lax.broadcasted_iota(jnp.int32, (rows + 2 * slots, rows), 0)
    spread = jnp.zeros((rows + 2 * slots, rows), F32)
    for k in range(faces):
        spread = spread + jnp.where(slot == nbr_ref[k : k + 1, :], coef_ref[k : k + 1, :], 0.0)
    own = spread[slots : slots + rows]
    halo_ref[...] = jnp.concatenate([spread[:slots], spread[slots + rows :]], axis=0).astype(BF16)
    own_ref[...] = own.astype(BF16)
    own_t = own.T.astype(BF16)
    for m in range(batches):
        x = x_ref[m]
        inner_ref[m] = dot(own_t, x)
        base_ref[m] = dot(x, w_ref[:width])


def forward_kernel(info_ref, base_ref, inner_ref, near_ref, far_ref, halo_ref, w_ref, slope_ref, act_ref, agg_ref):
    batches, rows, width = base_ref.shape
    slots = near_ref.shape[1]
    odd = odd_of(info_ref) == 1
    lower, upper = halo_ref[:slots].astype(F32), halo_ref[slots:].astype(F32)
    near = jnp.where(odd, lower, upper)
    far = jnp.where(end_of(info_ref) == 1, 0.0, jnp.where(odd, upper, lower))
    halo_t = jnp.concatenate([near, far], axis=0).T.astype(BF16)
    for m in range(batches):
        edge = jnp.concatenate([near_ref[m], far_ref[m]], axis=0)
        agg = (inner_ref[m] + dot(halo_t, edge)).astype(BF16)
        z = base_ref[m] + dot(agg, w_ref[width:])
        sig = 1.0 / (1.0 + jnp.exp(-z))
        agg_ref[m] = agg
        act_ref[m] = (z * sig).astype(BF16)
        slope_ref[m] = sig * (1.0 + z * (1.0 - sig))


def assemble(local, upper, lower, place):
    edge = jnp.concatenate([upper, lower], axis=0)
    return (local.astype(F32) + dot(place, edge)).astype(BF16)


def step(g, first, slope_ref, own_ref, halo_ref, w1_ref, w2_ref, local_ref, below_ref, above_ref, g_ref, dz_ref):
    rows, width = slope_ref.shape[1:]
    slots = halo_ref.shape[0] // 2
    count = len(g)
    d_act = dot(jnp.concatenate(g, axis=0), w2_ref[...], ((1,), (1,)))
    dz = [(d_act[j * rows : (j + 1) * rows] * slope_ref[first + j]).astype(BF16) for j in range(count)]
    dj = dot(jnp.concatenate(dz, axis=0), w1_ref[...], ((1,), (1,)))
    for j in range(count):
        part = dj[j * rows : (j + 1) * rows]
        dagg = part[:, width:].astype(BF16)
        local = g[j].astype(F32) + part[:, :width] + dot(own_ref[...], dagg)
        local_ref[j] = local.astype(BF16)
        edge = dot(halo_ref[...], dagg).astype(BF16)
        below_ref[j] = edge[:slots]
        above_ref[j] = edge[slots:]
        g_ref[j] = g[j]
        dz_ref[j] = dz[j]


def start_values(hop, first, count, inputs):
    if hop == 0:
        return [inputs[0][first + j] for j in range(count)]
    loc_ref, upper_ref, lower_ref, place_ref = inputs
    return [assemble(loc_ref[j], upper_ref[j], lower_ref[j], place_ref[...]) for j in range(count)]


def make_step_kernel(hop, first, count):
    def body(info_ref, *refs):
        inputs, arrays = refs[:-10], refs[-10:]

        @pl.when(hop_of(info_ref) == hop)
        def _():
            step(start_values(hop, first, count, inputs), first, *arrays)

    return body


def make_last_kernel(hop, first, count, earlier):
    def body(info_ref, *refs):
        (local_ref, g_ref, dz_ref, near_ref, far_ref, below_ref, above_ref) = refs[-7:]
        kept_below, kept_above = refs[-9:-7]
        edges = refs[-9 - 2 * earlier : -9]
        arrays = refs[-14 - 2 * earlier : -9 - 2 * earlier]
        inputs = refs[: -14 - 2 * earlier]
        odd = odd_of(info_ref) == 1

        def sort(below, above, where):
            near_ref[where] = jnp.where(odd, below, above)
            far_ref[where] = jnp.where(odd, above, below)

        @pl.when(hop_of(info_ref) == hop)
        def _():
            step(start_values(hop, first, count, inputs), first, *arrays,
                 local_ref, below_ref, above_ref, g_ref, dz_ref)
            for c in range(earlier):
                sort(edges[2 * c][...], edges[2 * c + 1][...], slice(c * count, (c + 1) * count))
            sort(below_ref[...], above_ref[...], slice(first, first + count))

        @pl.when(hop_of(info_ref) != hop)
        def _():
            sort(kept_below[...], kept_above[...], slice(0, first + count))

    return body


def gradients(sources, parts, out_ref, start=None):
    width = out_ref.shape[1]
    for n, source in enumerate(sources):
        total = 0.0 if start is None else start[n * width : (n + 1) * width]
        for first, size, g, dz in parts:
            rows = source.shape[1]
            left = source[first : first + size].reshape(size * rows, width)
            right = (g if n == 2 else dz)[...].reshape(size * rows, width)
            total = total + dot(left, right, ((0,), (0,)))
        out_ref[n * width : (n + 1) * width] = total


def make_partial_kernel(hops, chunks):
    def body(info_ref, x_ref, agg_ref, act_ref, *refs):
        part_ref, local_ref, below_ref, above_ref, g_ref, dz_ref, sems = refs[-7:]
        here = [refs[2 * c : 2 * c + 2] for c in range(chunks - 1)]
        pieces = refs[2 * chunks - 2 : -7]
        targets = (local_ref, below_ref, above_ref, g_ref, dz_ref)
        batches = x_ref.shape[0]
        count = batches // chunks

        def copies(hop):
            return [pltpu.make_async_copy(pieces[(hop * chunks + c) * 5 + n],
                                          targets[n].at[pl.ds(c * count, count)], sems.at[n, c])
                    for n in range(5) for c in range(chunks)]

        for hop in range(hops - 1):
            @pl.when(hop_of(info_ref) == hop)
            def _():
                for copy in copies(hop):
                    copy.start()

        if chunks > 1:
            @pl.when(hop_of(info_ref) == hops - 1)
            def _():
                parts = [(c * count, count, g, dz) for c, (g, dz) in enumerate(here)]
                gradients((x_ref, agg_ref, act_ref), parts, part_ref)
        else:
            @pl.when(hop_of(info_ref) == hops - 1)
            def _():
                part_ref[...] = jnp.zeros_like(part_ref)

        if hops > 1:
            @pl.when(hop_of(info_ref) != hops - 1)
            def _():
                for copy in copies(0):
                    copy.wait()
                gradients((x_ref, agg_ref, act_ref), [(0, batches, g_ref, dz_ref)], part_ref)

    return body


def make_weight_kernel(last, first, count):
    def body(info_ref, x_ref, agg_ref, act_ref, part_ref, g_ref, dz_ref, near_ref, keep_ref, give_ref, grad_ref):
        width = part_ref.shape[1]
        half = keep_ref.shape[0]
        odd = odd_of(info_ref)

        @pl.when(hop_of(info_ref) == last)
        def _():
            gradients((x_ref, agg_ref, act_ref), [(first, count, g_ref, dz_ref)], grad_ref, part_ref)

        @pl.when(hop_of(info_ref) != last)
        def _():
            grad_ref[...] = part_ref[...]

        keep_ref[...] = grad_ref[pl.ds(pl.multiple_of(odd * half, half), half)]
        give_ref[:half] = grad_ref[pl.ds(pl.multiple_of((1 - odd) * half, half), half)].astype(BF16)
        give_ref[half:] = near_ref[...].reshape(give_ref.shape[0] - half, width)

    return body


def add(a, b):
    return (a.astype(F32) + b.astype(F32)).astype(BF16)


def take_kernel(keep_ref, came_ref, far_ref, p_ref, q_ref):
    quarter = p_ref.shape[0]
    p_ref[...] = add(keep_ref[:quarter], came_ref[:quarter])
    q_ref[...] = add(keep_ref[quarter:], came_ref[quarter : 2 * quarter])


def split_kernel(info_ref, mine_ref, other_ref, first_ref, second_ref):
    half = mine_ref.shape[0]
    size = first_ref.shape[0]
    odd = odd_of(info_ref) == 1
    mine, other = mine_ref[...].astype(F32), other_ref[...].astype(F32)
    low = jnp.where(odd, other, mine)
    high = jnp.where(odd, mine, other)
    first_ref[:half] = low
    first_ref[half:] = high[: size - half]
    second_ref[...] = high[size - half :]


def make_finish_kernel(last):
    def body(info_ref, came_ref, far_ref, place_ref, loc_ref, *refs):
        here, out_ref = refs[:-1], refs[-1]
        odd, end = odd_of(info_ref) == 1, end_of(info_ref) == 1
        batches, slots = far_ref.shape[:2]
        count = batches // len(here)
        start = came_ref.shape[0] - batches * slots

        def write(local):
            for m in range(batches):
                near = came_ref[start + m * slots : start + (m + 1) * slots]
                far = jnp.where(end, jnp.zeros_like(far_ref[m]), far_ref[m])
                upper = jnp.where(odd, far, near)
                lower = jnp.where(odd, near, far)
                out_ref[m] = assemble(local(m), upper, lower, place_ref[...])

        @pl.when(hop_of(info_ref) == last)
        def _():
            write(lambda m: here[m // count][m % count])

        @pl.when(hop_of(info_ref) != last)
        def _():
            write(lambda m: loc_ref[m])

    return body


def per_device(saved_inputs, grad_out, w_first, w_second, face_weight, neighbours, send_rows):
    x = saved_inputs[0]
    w1 = w_first[0]
    w2 = w_second[0]
    batches, rows, width = x.shape
    slots = send_rows.shape[1]
    sections = lax.axis_size("section")
    doms = lax.axis_size("dom")
    chunks = CHUNKS if batches % CHUNKS == 0 else 1
    count = batches // chunks
    dom = lax.axis_index("dom")
    hop_here = sections - 1 - lax.axis_index("section")
    end = ((dom == 0) | (dom == doms - 1)).astype(jnp.int32)
    info = (4 * hop_here + 2 * (dom % 2) + end).astype(jnp.int32).reshape(1)
    sds = jax.ShapeDtypeStruct
    smem = pl.BlockSpec(memory_space=pltpu.SMEM)
    any_spec = pl.BlockSpec(memory_space=pl.ANY)
    hbm_spec = pl.BlockSpec(memory_space=pltpu.HBM)

    def like(value):
        return sds(value.shape, value.dtype)

    def call(body, outs, *args, scratch=(), name):
        return pl.pallas_call(
            body, in_specs=[smem] + [vmem()] * (len(args) - 1), out_specs=[vmem()] * len(outs), out_shape=outs,
            scratch_shapes=scratch, compiler_params=params(), name=name,
        )(*args)

    near_pairs = [(p, p ^ 1) for p in range(doms)]
    far_pairs = [(p, (p + 1 if p % 2 else p - 1) % doms) for p in range(doms)]

    edge_shape = sds((batches, slots, width), BF16)
    x, grad_out, w1, w2, neighbours, face_weight, place, near, far = pl.pallas_call(
        load_kernel,
        in_specs=[smem] + [hbm_spec] * 7,
        out_specs=[vmem()] * 9,
        out_shape=(like(x), like(grad_out), like(w1), like(w2), like(neighbours), like(face_weight),
                   sds((rows, 2 * slots), BF16), edge_shape, edge_shape),
        scratch_shapes=[pltpu.VMEM(send_rows.shape, send_rows.dtype), pltpu.SemaphoreType.DMA((7,))],
        compiler_params=params(), name="load",
    )(info, *[pltpu.with_memory_space_constraint(value, pltpu.HBM)
             for value in (x, grad_out, w1, w2, neighbours, face_weight, send_rows)])
    near, far = lax.ppermute(near, "dom", near_pairs), lax.ppermute(far, "dom", far_pairs)

    full_shape = sds((batches, rows, width), BF16)
    wide_shape = sds((batches, rows, width), F32)
    base, inner, own, halo = pl.pallas_call(
        inner_kernel, in_specs=[vmem()] * 4, out_specs=[vmem()] * 4,
        out_shape=(wide_shape, wide_shape, sds((rows, rows), BF16), sds((2 * slots, rows), BF16)),
        compiler_params=params(), name="inner",
    )(x, neighbours, face_weight, w1)
    slope, act, agg = call(
        forward_kernel, (wide_shape, full_shape, full_shape), info, base, inner, near, far, halo, w1, name="forward")

    def move(value, hop, shift):
        source = sections - 1 - hop
        pairs = [(p * sections + source, (p + shift) * sections + source - 1)
                 for p in range(doms) if 0 <= p + shift < doms]
        return lax.ppermute(value, ("dom", "section"), pairs)

    piece, piece_edge = sds((count, rows, width), BF16), sds((count, slots, width), BF16)
    estimate = pl.CostEstimate(flops=STEP_FLOPS, bytes_accessed=1 << 20, transcendentals=0)
    pieces = []
    received = [None] * chunks
    weights = (slope, own, halo, w1, w2)
    for hop in range(sections):
        sent = []
        for c in range(chunks):
            inputs = (grad_out,) if hop == 0 else (*received[c], place)
            if hop + 1 == sections and c + 1 == chunks:
                break
            local, to_below, to_above, g, dz = pl.pallas_call(
                make_step_kernel(hop, c * count, count),
                in_specs=[smem] + [vmem()] * (len(inputs) + 5), out_specs=[vmem()] * 5,
                out_shape=(piece, piece_edge, piece_edge, piece, piece),
                cost_estimate=estimate, compiler_params=params(), name="step",
            )(info, *inputs, *weights)
            pieces.append((local, to_below, to_above, g, dz))
            if hop + 1 < sections:
                sent.append((move(local, hop, 0), move(to_below, hop, -1), move(to_above, hop, 1)))
        received = sent if sent else received

    early = chunks - 1
    here, others = pieces[len(pieces) - early :], pieces[: len(pieces) - early]
    last = sections - 1
    part, local, kept_below, kept_above = pl.pallas_call(
        make_partial_kernel(sections, chunks),
        in_specs=[smem] + [vmem()] * (3 + 2 * early) + [any_spec] * (5 * len(others)),
        out_specs=[vmem()] * 4,
        out_shape=(sds((3 * width, width), F32), full_shape, edge_shape, edge_shape),
        scratch_shapes=[pltpu.VMEM(full_shape.shape, BF16)] * 2 + [pltpu.SemaphoreType.DMA((5, chunks))],
        compiler_params=params(), name="partial",
    )(info, x, agg, act, *[value for outs in here for value in outs[3:]],
      *[value for outs in others for value in outs])
    edges = [value for outs in here for value in outs[1:3]]
    local_last, g, dz, near, far = pl.pallas_call(
        make_last_kernel(last, early * count, count, early),
        in_specs=[smem] + [vmem()] * (len(inputs) + 7 + 2 * early), out_specs=[vmem()] * 5,
        out_shape=(piece, piece, piece, edge_shape, edge_shape),
        scratch_shapes=[pltpu.VMEM(piece_edge.shape, BF16)] * 2,
        cost_estimate=estimate, compiler_params=params(), name="step_last",
    )(info, *inputs, *weights, *edges, kept_below, kept_above)
    far = lax.ppermute(far, "dom", far_pairs)
    half = 3 * width // 2
    keep, give = pl.pallas_call(
        make_weight_kernel(last, early * count, count), in_specs=[smem] + [vmem()] * 7, out_specs=[vmem()] * 2,
        out_shape=(sds((half, width), F32), sds((half + batches * slots, width), BF16)),
        scratch_shapes=[pltpu.VMEM((3 * width, width), F32)],
        cost_estimate=estimate, compiler_params=params(), name="weights",
    )(info, x, agg, act, part, g, dz, near)

    def swap(value, mask):
        return lax.ppermute(value, "dom", [(i, i ^ mask) for i in range(doms)])

    came = swap(give, 1)
    quarter = sds((half // 2, width), BF16)
    p, q = pl.pallas_call(
        take_kernel, in_specs=[vmem()] * 2 + [any_spec], out_specs=[vmem()] * 2, out_shape=(quarter, quarter),
        compiler_params=params(), name="take",
    )(keep, came, far)
    bit = 2
    while bit < doms:
        if bit * 2 < doms:
            p, q = add(p, swap(p, bit)), add(q, swap(q, 2 * bit))
            p, q = add(p, swap(p, 2 * bit)), add(q, swap(q, bit))
        else:
            p, q = add(p, swap(p, bit)), add(q, swap(q, bit))
        bit *= 4
    mine = jnp.concatenate([p, q], axis=0)
    other = swap(mine, 1)
    grad_in = pl.pallas_call(
        make_finish_kernel(last), in_specs=[smem] + [vmem()] * (4 + chunks), out_specs=vmem(),
        out_shape=full_shape, compiler_params=params(), name="finish",
    )(info, came, far, place, local, *[outs[0] for outs in here], local_last)
    first, second = call(
        split_kernel, (sds((2 * width, width), F32), sds((width, width), F32)), info, mine, other, name="split")
    return grad_in[None], first[None], second[None]


def solution(mesh):
    return jax.shard_map(
        per_device,
        mesh=mesh,
        in_specs=(
            P("section", None, "dom", None),
            P(None, "dom", None),
            P("section", None, None),
            P("section", None, None),
            P(None, "dom"),
            P(None, "dom"),
            P(None, "dom"),
        ),
        out_specs=(
            P("section", None, "dom", None),
            P("section", None, None),
            P("section", None, None),
        ),
        check_vma=False,
    )
```

```python
import functools

import jax
import jax.numpy as jnp
from jax import lax
from jax.experimental import pallas as pl
from jax.experimental.pallas import tpu as pltpu
from jax.sharding import PartitionSpec as P

F32 = jnp.float32
BF16 = jnp.bfloat16
CHUNKS = 2
STEP_FLOPS = 10**11


def dot(a, b, dims=((1,), (0,))):
    return lax.dot_general(a, b, (dims, ((), ())), preferred_element_type=F32)


def hop_of(info_ref):
    return info_ref[0] >> 3


def direct_of(info_ref):
    return (info_ref[0] >> 2) & 1


def odd_of(info_ref):
    return (info_ref[0] >> 1) & 1


def end_of(info_ref):
    return info_ref[0] & 1


def vmem():
    return pl.BlockSpec(memory_space=pltpu.VMEM)


def params():
    return pltpu.CompilerParams(vmem_limit_bytes=16 * 1024 * 1024)


def load_kernel(info_ref, x_hbm, g_hbm, w1_hbm, w2_hbm, nbr_hbm, coef_hbm, send_hbm,
                x_ref, g_ref, w1_ref, w2_ref, nbr_ref, coef_ref, place_ref, near_ref, far_ref, send_ref, sems):
    sources = (send_hbm, x_hbm, nbr_hbm, coef_hbm, w1_hbm, w2_hbm, g_hbm)
    targets = (send_ref, x_ref, nbr_ref, coef_ref, w1_ref, w2_ref, g_ref)
    copies = [pltpu.make_async_copy(source, target, sems.at[n])
              for n, (source, target) in enumerate(zip(sources, targets))]
    for copy in copies:
        copy.start()
    batches, rows, _ = x_ref.shape
    slots = send_ref.shape[1]
    row = lax.broadcasted_iota(jnp.int32, (rows, slots), 0)
    copies[0].wait()
    up = jnp.where(row == send_ref[0:1, :], 1.0, 0.0)
    down = jnp.where(row == send_ref[1:2, :], 1.0, 0.0)
    place = jnp.concatenate([up, down], axis=1)
    place_ref[...] = place.astype(BF16)
    pick = place.T.astype(BF16)
    copies[1].wait()
    odd = odd_of(info_ref) == 1
    for m in range(batches):
        sent = dot(pick, x_ref[m])
        up, down = sent[:slots], sent[slots:]
        near_ref[m] = jnp.where(odd, down, up).astype(BF16)
        far_ref[m] = jnp.where(odd, up, down).astype(BF16)
    for copy in copies[2:]:
        copy.wait()


def inner_kernel(x_ref, nbr_ref, coef_ref, w_ref, base_ref, inner_ref, own_ref, halo_ref):
    batches, rows, width = x_ref.shape
    slots = halo_ref.shape[0] // 2
    faces = nbr_ref.shape[0]
    slot = lax.broadcasted_iota(jnp.int32, (rows + 2 * slots, rows), 0)
    spread = jnp.zeros((rows + 2 * slots, rows), F32)
    for k in range(faces):
        spread = spread + jnp.where(slot == nbr_ref[k : k + 1, :], coef_ref[k : k + 1, :], 0.0)
    own = spread[slots : slots + rows]
    halo_ref[...] = jnp.concatenate([spread[:slots], spread[slots + rows :]], axis=0).astype(BF16)
    own_ref[...] = own.astype(BF16)
    own_t = own.T.astype(BF16)
    for m in range(batches):
        x = x_ref[m]
        inner_ref[m] = dot(own_t, x)
        base_ref[m] = dot(x, w_ref[:width])


def forward_kernel(info_ref, base_ref, inner_ref, near_ref, far_ref, halo_ref, w_ref, slope_ref, act_ref, agg_ref):
    batches, rows, width = base_ref.shape
    slots = near_ref.shape[1]
    odd = odd_of(info_ref) == 1
    lower, upper = halo_ref[:slots].astype(F32), halo_ref[slots:].astype(F32)
    near = jnp.where(odd, lower, upper)
    far = jnp.where(end_of(info_ref) == 1, 0.0, jnp.where(odd, upper, lower))
    halo_t = jnp.concatenate([near, far], axis=0).T.astype(BF16)
    for m in range(batches):
        edge = jnp.concatenate([near_ref[m], far_ref[m]], axis=0)
        agg = (inner_ref[m] + dot(halo_t, edge)).astype(BF16)
        z = base_ref[m] + dot(agg, w_ref[width:])
        sig = 1.0 / (1.0 + jnp.exp(-z))
        agg_ref[m] = agg
        act_ref[m] = (z * sig).astype(BF16)
        slope_ref[m] = sig * (1.0 + z * (1.0 - sig))


def assemble(local, upper, lower, place):
    edge = jnp.concatenate([upper, lower], axis=0)
    return (local.astype(F32) + dot(place, edge)).astype(BF16)


def step(g, first, slope_ref, own_ref, halo_ref, w1_ref, w2_ref, local_ref, below_ref, above_ref, g_ref, dz_ref):
    rows, width = slope_ref.shape[1:]
    slots = halo_ref.shape[0] // 2
    count = len(g)
    d_act = dot(jnp.concatenate(g, axis=0), w2_ref[...], ((1,), (1,)))
    dz = [(d_act[j * rows : (j + 1) * rows] * slope_ref[first + j]).astype(BF16) for j in range(count)]
    dj = dot(jnp.concatenate(dz, axis=0), w1_ref[...], ((1,), (1,)))
    for j in range(count):
        part = dj[j * rows : (j + 1) * rows]
        dagg = part[:, width:].astype(BF16)
        local = g[j].astype(F32) + part[:, :width] + dot(own_ref[...], dagg)
        local_ref[j] = local.astype(BF16)
        edge = dot(halo_ref[...], dagg).astype(BF16)
        below_ref[j] = edge[:slots]
        above_ref[j] = edge[slots:]
        g_ref[j] = g[j]
        dz_ref[j] = dz[j]


def start_values(hop, first, count, inputs):
    if hop == 0:
        return [inputs[0][first + j] for j in range(count)]
    loc_ref, upper_ref, lower_ref, place_ref = inputs
    return [assemble(loc_ref[j], upper_ref[j], lower_ref[j], place_ref[...]) for j in range(count)]


def make_step_kernel(hop, first, count):
    def body(info_ref, *refs):
        inputs, arrays = refs[:-10], refs[-10:]

        @pl.when(hop_of(info_ref) == hop)
        def _():
            step(start_values(hop, first, count, inputs), first, *arrays)

    return body


def make_last_kernel(hop, first, count, earlier):
    def body(info_ref, *refs):
        (local_ref, g_ref, dz_ref, near_ref, far_ref, below_ref, above_ref) = refs[-7:]
        kept_below, kept_above = refs[-9:-7]
        edges = refs[-9 - 2 * earlier : -9]
        arrays = refs[-14 - 2 * earlier : -9 - 2 * earlier]
        inputs = refs[: -14 - 2 * earlier]
        odd = odd_of(info_ref) == 1

        def sort(below, above, where):
            near_ref[where] = jnp.where(odd, below, above)
            far_ref[where] = jnp.where(odd, above, below)

        @pl.when(hop_of(info_ref) == hop)
        def _():
            step(start_values(hop, first, count, inputs), first, *arrays,
                 local_ref, below_ref, above_ref, g_ref, dz_ref)
            for c in range(earlier):
                sort(edges[2 * c][...], edges[2 * c + 1][...], slice(c * count, (c + 1) * count))
            sort(below_ref[...], above_ref[...], slice(first, first + count))

        @pl.when(hop_of(info_ref) != hop)
        def _():
            sort(kept_below[...], kept_above[...], slice(0, first + count))

    return body


def gradients(sources, parts, out_ref, start=None):
    width = out_ref.shape[1]
    for n, source in enumerate(sources):
        total = 0.0 if start is None else start[n * width : (n + 1) * width]
        for first, size, g, dz in parts:
            rows = source.shape[1]
            left = source[first : first + size].reshape(size * rows, width)
            right = (g if n == 2 else dz)[...].reshape(size * rows, width)
            total = total + dot(left, right, ((0,), (0,)))
        out_ref[n * width : (n + 1) * width] = total


def make_partial_kernel(hops, chunks):
    def body(info_ref, x_ref, agg_ref, act_ref, *refs):
        part_ref, local_ref, below_ref, above_ref, g_ref, dz_ref, sems = refs[-7:]
        here = [refs[2 * c : 2 * c + 2] for c in range(chunks - 1)]
        pieces = refs[2 * chunks - 2 : -7]
        targets = (local_ref, below_ref, above_ref, g_ref, dz_ref)
        batches = x_ref.shape[0]
        count = batches // chunks

        def copies(hop):
            return [pltpu.make_async_copy(pieces[(hop * chunks + c) * 5 + n],
                                          targets[n].at[pl.ds(c * count, count)], sems.at[n, c])
                    for n in range(5) for c in range(chunks)]

        for hop in range(hops - 1):
            @pl.when(hop_of(info_ref) == hop)
            def _():
                for copy in copies(hop):
                    copy.start()

        if chunks > 1:
            @pl.when(hop_of(info_ref) == hops - 1)
            def _():
                parts = [(c * count, count, g, dz) for c, (g, dz) in enumerate(here)]
                gradients((x_ref, agg_ref, act_ref), parts, part_ref)
        else:
            @pl.when(hop_of(info_ref) == hops - 1)
            def _():
                part_ref[...] = jnp.zeros_like(part_ref)

        if hops > 1:
            @pl.when(hop_of(info_ref) != hops - 1)
            def _():
                for copy in copies(0):
                    copy.wait()
                gradients((x_ref, agg_ref, act_ref), [(0, batches, g_ref, dz_ref)], part_ref)

    return body


def make_weight_kernel(last, first, count):
    def body(info_ref, x_ref, agg_ref, act_ref, part_ref, g_ref, dz_ref, near_ref, far_ref, keep_ref, give_ref, grad_ref):
        width = part_ref.shape[1]
        half = keep_ref.shape[0]
        odd = odd_of(info_ref)

        @pl.when(hop_of(info_ref) == last)
        def _():
            gradients((x_ref, agg_ref, act_ref), [(first, count, g_ref, dz_ref)], grad_ref, part_ref)

        @pl.when(hop_of(info_ref) != last)
        def _():
            grad_ref[...] = part_ref[...]

        keep_ref[...] = grad_ref[pl.ds(pl.multiple_of(odd * half, half), half)]
        give_ref[:half] = grad_ref[pl.ds(pl.multiple_of((1 - odd) * half, half), half)].astype(BF16)
        size = near_ref.shape[0] * near_ref.shape[1]
        give_ref[half : half + size] = near_ref[...].reshape(size, width)
        if give_ref.shape[0] > half + size:
            give_ref[half + size :] = far_ref[...].reshape(size, width)

    return body


def add(a, b):
    return (a.astype(F32) + b.astype(F32)).astype(BF16)


def take_kernel(keep_ref, came_ref, far_ref, p_ref, q_ref):
    quarter = q_ref.shape[0]
    p_ref[:quarter] = add(keep_ref[:quarter], came_ref[:quarter])
    q_ref[...] = add(keep_ref[quarter:], came_ref[quarter : 2 * quarter])
    extra = p_ref.shape[0] - quarter
    if extra:
        p_ref[quarter:] = came_ref[came_ref.shape[0] - extra :]


def forward_sum_kernel(p_ref, other_ref, out_ref, *, quarter):
    out_ref[:quarter] = add(p_ref[:quarter], other_ref[:quarter])
    out_ref[quarter:] = other_ref[quarter:]


def join_kernel(p_ref, p_other_ref, q_ref, q_other_ref, out_ref):
    quarter = q_ref.shape[0]
    out_ref[:quarter] = add(p_ref[:quarter], p_other_ref[:quarter])
    out_ref[quarter:] = add(q_ref[...], q_other_ref[...])


def split_kernel(info_ref, mine_ref, other_ref, first_ref, second_ref):
    half = mine_ref.shape[0]
    size = first_ref.shape[0]
    odd = odd_of(info_ref) == 1
    mine, other = mine_ref[...].astype(F32), other_ref[...].astype(F32)
    low = jnp.where(odd, other, mine)
    high = jnp.where(odd, mine, other)
    first_ref[:half] = low
    first_ref[half:] = high[: size - half]
    second_ref[...] = high[size - half :]


def make_finish_kernel(last, half, slots, relay):
    def body(info_ref, came_ref, place_ref, loc_ref, *refs):
        here, halos, out_ref = refs[: -2 - relay], refs[-2 - relay : -1], refs[-1]
        odd, end = odd_of(info_ref) == 1, end_of(info_ref) == 1
        batches = loc_ref.shape[0]
        count = batches // len(here)

        def far_of(m):
            if not relay:
                return halos[0][m]
            first, second = [halo[halo.shape[0] - (batches - m) * slots :][:slots] for halo in halos]
            return jnp.where(direct_of(info_ref) == 1, first, second)

        def write(local):
            for m in range(batches):
                near = came_ref[half + m * slots : half + (m + 1) * slots]
                far = far_of(m)
                far = jnp.where(end, jnp.zeros_like(far), far)
                upper = jnp.where(odd, far, near)
                lower = jnp.where(odd, near, far)
                out_ref[m] = assemble(local(m), upper, lower, place_ref[...])

        @pl.when(hop_of(info_ref) == last)
        def _():
            write(lambda m: here[m // count][m % count])

        @pl.when(hop_of(info_ref) != last)
        def _():
            write(lambda m: loc_ref[m])

    return body


def per_device(saved_inputs, grad_out, w_first, w_second, face_weight, neighbours, send_rows):
    x = saved_inputs[0]
    w1 = w_first[0]
    w2 = w_second[0]
    batches, rows, width = x.shape
    slots = send_rows.shape[1]
    sections = lax.axis_size("section")
    doms = lax.axis_size("dom")
    chunks = CHUNKS if batches % CHUNKS == 0 else 1
    count = batches // chunks
    dom = lax.axis_index("dom")
    hop_here = sections - 1 - lax.axis_index("section")
    end = ((dom == 0) | (dom == doms - 1)).astype(jnp.int32)
    direct = ((dom + 1) % 4 >= 2).astype(jnp.int32)
    info = (8 * hop_here + 4 * direct + 2 * (dom % 2) + end).astype(jnp.int32).reshape(1)
    sds = jax.ShapeDtypeStruct
    smem = pl.BlockSpec(memory_space=pltpu.SMEM)
    any_spec = pl.BlockSpec(memory_space=pl.ANY)
    hbm_spec = pl.BlockSpec(memory_space=pltpu.HBM)

    def like(value):
        return sds(value.shape, value.dtype)

    def call(body, outs, *args, scratch=(), name):
        return pl.pallas_call(
            body, in_specs=[smem] + [vmem()] * (len(args) - 1), out_specs=[vmem()] * len(outs), out_shape=outs,
            scratch_shapes=scratch, compiler_params=params(), name=name,
        )(*args)

    near_pairs = [(p, p ^ 1) for p in range(doms)]
    far_pairs = [(p, (p + 1 if p % 2 else p - 1) % doms) for p in range(doms)]

    edge_shape = sds((batches, slots, width), BF16)
    x, grad_out, w1, w2, neighbours, face_weight, place, near, far = pl.pallas_call(
        load_kernel,
        in_specs=[smem] + [hbm_spec] * 7,
        out_specs=[vmem()] * 9,
        out_shape=(like(x), like(grad_out), like(w1), like(w2), like(neighbours), like(face_weight),
                   sds((rows, 2 * slots), BF16), edge_shape, edge_shape),
        scratch_shapes=[pltpu.VMEM(send_rows.shape, send_rows.dtype), pltpu.SemaphoreType.DMA((7,))],
        compiler_params=params(), name="load",
    )(info, *[pltpu.with_memory_space_constraint(value, pltpu.HBM)
             for value in (x, grad_out, w1, w2, neighbours, face_weight, send_rows)])
    near, far = lax.ppermute(near, "dom", near_pairs), lax.ppermute(far, "dom", far_pairs)

    full_shape = sds((batches, rows, width), BF16)
    wide_shape = sds((batches, rows, width), F32)
    base, inner, own, halo = pl.pallas_call(
        inner_kernel, in_specs=[vmem()] * 4, out_specs=[vmem()] * 4,
        out_shape=(wide_shape, wide_shape, sds((rows, rows), BF16), sds((2 * slots, rows), BF16)),
        compiler_params=params(), name="inner",
    )(x, neighbours, face_weight, w1)
    slope, act, agg = call(
        forward_kernel, (wide_shape, full_shape, full_shape), info, base, inner, near, far, halo, w1, name="forward")

    def move(value, hop, shift):
        source = sections - 1 - hop
        pairs = [(p * sections + source, (p + shift) * sections + source - 1)
                 for p in range(doms) if 0 <= p + shift < doms]
        return lax.ppermute(value, ("dom", "section"), pairs)

    piece, piece_edge = sds((count, rows, width), BF16), sds((count, slots, width), BF16)
    estimate = pl.CostEstimate(flops=STEP_FLOPS, bytes_accessed=1 << 20, transcendentals=0)
    pieces = []
    received = [None] * chunks
    weights = (slope, own, halo, w1, w2)
    for hop in range(sections):
        sent = []
        for c in range(chunks):
            inputs = (grad_out,) if hop == 0 else (*received[c], place)
            if hop + 1 == sections and c + 1 == chunks:
                break
            local, to_below, to_above, g, dz = pl.pallas_call(
                make_step_kernel(hop, c * count, count),
                in_specs=[smem] + [vmem()] * (len(inputs) + 5), out_specs=[vmem()] * 5,
                out_shape=(piece, piece_edge, piece_edge, piece, piece),
                cost_estimate=estimate, compiler_params=params(), name="step",
            )(info, *inputs, *weights)
            pieces.append((local, to_below, to_above, g, dz))
            if hop + 1 < sections:
                sent.append((move(local, hop, 0), move(to_below, hop, -1), move(to_above, hop, 1)))
        received = sent if sent else received

    early = chunks - 1
    here, others = pieces[len(pieces) - early :], pieces[: len(pieces) - early]
    last = sections - 1
    part, local, kept_below, kept_above = pl.pallas_call(
        make_partial_kernel(sections, chunks),
        in_specs=[smem] + [vmem()] * (3 + 2 * early) + [any_spec] * (5 * len(others)),
        out_specs=[vmem()] * 4,
        out_shape=(sds((3 * width, width), F32), full_shape, edge_shape, edge_shape),
        scratch_shapes=[pltpu.VMEM(full_shape.shape, BF16)] * 2 + [pltpu.SemaphoreType.DMA((5, chunks))],
        compiler_params=params(), name="partial",
    )(info, x, agg, act, *[value for outs in here for value in outs[3:]],
      *[value for outs in others for value in outs])
    edges = [value for outs in here for value in outs[1:3]]
    local_last, g, dz, near, far = pl.pallas_call(
        make_last_kernel(last, early * count, count, early),
        in_specs=[smem] + [vmem()] * (len(inputs) + 7 + 2 * early), out_specs=[vmem()] * 5,
        out_shape=(piece, piece, piece, edge_shape, edge_shape),
        scratch_shapes=[pltpu.VMEM(piece_edge.shape, BF16)] * 2,
        cost_estimate=estimate, compiler_params=params(), name="step_last",
    )(info, *inputs, *weights, *edges, kept_below, kept_above)
    relay = doms == 8
    half = 3 * width // 2
    size = batches * slots
    keep, give = pl.pallas_call(
        make_weight_kernel(last, early * count, count), in_specs=[smem] + [vmem()] * 8, out_specs=[vmem()] * 2,
        out_shape=(sds((half, width), F32), sds((half + (1 + relay) * size, width), BF16)),
        scratch_shapes=[pltpu.VMEM((3 * width, width), F32)],
        cost_estimate=estimate, compiler_params=params(), name="weights",
    )(info, x, agg, act, part, g, dz, near, far)
    if not relay:
        far = lax.ppermute(far, "dom", far_pairs)

    def swap(value, mask):
        return lax.ppermute(value, "dom", [(i, i ^ mask) for i in range(doms)])

    came = swap(give, 1)
    quarter = sds((half // 2, width), BF16)
    longer = sds((half // 2 + relay * size, width), BF16)
    p, q = pl.pallas_call(
        take_kernel, in_specs=[vmem()] * 2 + [any_spec], out_specs=[vmem()] * 2, out_shape=(longer, quarter),
        compiler_params=params(), name="take",
    )(keep, came, far)
    halos = [] if relay else [far]
    bit = 2
    while bit < doms:
        if bit * 2 < doms:
            p_other, q_other = swap(p, bit), swap(q, 2 * bit)
            if relay:
                halos.append(p_other)
                p = pl.pallas_call(
                    functools.partial(forward_sum_kernel, quarter=half // 2), in_specs=[vmem()] * 2, out_specs=vmem(),
                    out_shape=longer, compiler_params=params(), name="forward_sum",
                )(p, p_other)
            else:
                p = add(p, p_other)
            q = add(q, q_other)
            p_other, q_other = swap(p, 2 * bit), swap(q, bit)
            if relay:
                halos.append(p_other)
        else:
            p_other, q_other = swap(p, bit), swap(q, bit)
        bit *= 4
        if bit < doms:
            p, q = add(p, p_other), add(q, q_other)
    mine = pl.pallas_call(
        join_kernel, in_specs=[vmem()] * 4, out_specs=vmem(), out_shape=sds((half, width), BF16),
        compiler_params=params(), name="join",
    )(p, p_other, q, q_other)
    other = swap(mine, 1)
    grad_in = pl.pallas_call(
        make_finish_kernel(last, half, slots, relay), in_specs=[smem] + [vmem()] * (3 + chunks + len(halos)),
        out_specs=vmem(), out_shape=full_shape, compiler_params=params(), name="finish",
    )(info, came, place, local, *[outs[0] for outs in here], local_last, *halos)
    first, second = call(
        split_kernel, (sds((2 * width, width), F32), sds((width, width), F32)), info, mine, other, name="split")
    return grad_in[None], first[None], second[None]


def solution(mesh):
    return jax.shard_map(
        per_device,
        mesh=mesh,
        in_specs=(
            P("section", None, "dom", None),
            P(None, "dom", None),
            P("section", None, None),
            P("section", None, None),
            P(None, "dom"),
            P(None, "dom"),
            P(None, "dom"),
        ),
        out_specs=(
            P("section", None, "dom", None),
            P("section", None, None),
            P("section", None, None),
        ),
        check_vma=False,
    )
```

```python
import functools

import jax
import jax.numpy as jnp
from jax import lax
from jax.experimental import pallas as pl
from jax.experimental.pallas import tpu as pltpu
from jax.sharding import PartitionSpec as P

F32 = jnp.float32
BF16 = jnp.bfloat16
CHUNKS = 2
STEP_FLOPS = 2600 * 10**6


def dot(a, b, dims=((1,), (0,))):
    return lax.dot_general(a, b, (dims, ((), ())), preferred_element_type=F32)


def hop_of(info_ref):
    return info_ref[0] >> 3


def direct_of(info_ref):
    return (info_ref[0] >> 2) & 1


def odd_of(info_ref):
    return (info_ref[0] >> 1) & 1


def end_of(info_ref):
    return info_ref[0] & 1


def vmem():
    return pl.BlockSpec(memory_space=pltpu.VMEM)


def params():
    return pltpu.CompilerParams(vmem_limit_bytes=16 * 1024 * 1024)


def load_kernel(info_ref, x_hbm, g_hbm, w1_hbm, w2_hbm, nbr_hbm, coef_hbm, send_hbm,
                x_ref, g_ref, w1_ref, w2_ref, nbr_ref, coef_ref, place_ref, near_ref, far_ref, send_ref, sems):
    sources = (send_hbm, x_hbm, nbr_hbm, coef_hbm, w1_hbm, w2_hbm, g_hbm)
    targets = (send_ref, x_ref, nbr_ref, coef_ref, w1_ref, w2_ref, g_ref)
    copies = [pltpu.make_async_copy(source, target, sems.at[n])
              for n, (source, target) in enumerate(zip(sources, targets))]
    for copy in copies:
        copy.start()
    batches, rows, _ = x_ref.shape
    slots = send_ref.shape[1]
    row = lax.broadcasted_iota(jnp.int32, (rows, slots), 0)
    copies[0].wait()
    up = jnp.where(row == send_ref[0:1, :], 1.0, 0.0)
    down = jnp.where(row == send_ref[1:2, :], 1.0, 0.0)
    place = jnp.concatenate([up, down], axis=1)
    place_ref[...] = place.astype(BF16)
    pick = place.T.astype(BF16)
    copies[1].wait()
    odd = odd_of(info_ref) == 1
    for m in range(batches):
        sent = dot(pick, x_ref[m])
        up, down = sent[:slots], sent[slots:]
        near_ref[m] = jnp.where(odd, down, up).astype(BF16)
        far_ref[m] = jnp.where(odd, up, down).astype(BF16)
    for copy in copies[2:]:
        copy.wait()


def inner_kernel(x_ref, nbr_ref, coef_ref, w_ref, base_ref, inner_ref, own_ref, halo_ref):
    batches, rows, width = x_ref.shape
    slots = halo_ref.shape[0] // 2
    faces = nbr_ref.shape[0]
    slot = lax.broadcasted_iota(jnp.int32, (rows + 2 * slots, rows), 0)
    spread = jnp.zeros((rows + 2 * slots, rows), F32)
    for k in range(faces):
        spread = spread + jnp.where(slot == nbr_ref[k : k + 1, :], coef_ref[k : k + 1, :], 0.0)
    own = spread[slots : slots + rows]
    halo_ref[...] = jnp.concatenate([spread[:slots], spread[slots + rows :]], axis=0).astype(BF16)
    own_ref[...] = own.astype(BF16)
    own_t = own.T.astype(BF16)
    for m in range(batches):
        x = x_ref[m]
        inner_ref[m] = dot(own_t, x)
        base_ref[m] = dot(x, w_ref[:width])


def make_forward_kernel(first):
    def body(info_ref, base_ref, inner_ref, near_ref, far_ref, halo_ref, w_ref, slope_ref, act_ref, agg_ref):
        width = base_ref.shape[2]
        slots = near_ref.shape[1]
        odd = odd_of(info_ref) == 1
        lower, upper = halo_ref[:slots].astype(F32), halo_ref[slots:].astype(F32)
        near = jnp.where(odd, lower, upper)
        far = jnp.where(end_of(info_ref) == 1, 0.0, jnp.where(odd, upper, lower))
        halo_t = jnp.concatenate([near, far], axis=0).T.astype(BF16)
        for j in range(slope_ref.shape[0]):
            m = first + j
            edge = jnp.concatenate([near_ref[m], far_ref[m]], axis=0)
            agg = (inner_ref[m] + dot(halo_t, edge)).astype(BF16)
            z = base_ref[m] + dot(agg, w_ref[width:])
            sig = 1.0 / (1.0 + jnp.exp(-z))
            agg_ref[j] = agg
            act_ref[j] = (z * sig).astype(BF16)
            slope_ref[j] = sig * (1.0 + z * (1.0 - sig))

    return body


def assemble(local, upper, lower, place):
    edge = jnp.concatenate([upper, lower], axis=0)
    return (local.astype(F32) + dot(place, edge)).astype(BF16)


def step(g, slope_ref, own_ref, halo_ref, w1_ref, w2_ref, local_ref, below_ref, above_ref, g_ref, dz_ref):
    rows, width = slope_ref.shape[1:]
    slots = halo_ref.shape[0] // 2
    count = len(g)
    d_act = dot(jnp.concatenate(g, axis=0), w2_ref[...], ((1,), (1,)))
    dz = [(d_act[j * rows : (j + 1) * rows] * slope_ref[j]).astype(BF16) for j in range(count)]
    dj = dot(jnp.concatenate(dz, axis=0), w1_ref[...], ((1,), (1,)))
    for j in range(count):
        part = dj[j * rows : (j + 1) * rows]
        dagg = part[:, width:].astype(BF16)
        local = g[j].astype(F32) + part[:, :width] + dot(own_ref[...], dagg)
        local_ref[j] = local.astype(BF16)
        edge = dot(halo_ref[...], dagg).astype(BF16)
        below_ref[j] = edge[:slots]
        above_ref[j] = edge[slots:]
        g_ref[j] = g[j]
        dz_ref[j] = dz[j]


def start_values(hop, first, count, inputs):
    if hop == 0:
        return [inputs[0][first + j] for j in range(count)]
    loc_ref, upper_ref, lower_ref, place_ref = inputs
    return [assemble(loc_ref[j], upper_ref[j], lower_ref[j], place_ref[...]) for j in range(count)]


def make_step_kernel(hop, first, count):
    def body(info_ref, *refs):
        inputs, arrays = refs[:-10], refs[-10:]

        @pl.when(hop_of(info_ref) == hop)
        def _():
            step(start_values(hop, first, count, inputs), *arrays)

    return body


def make_last_kernel(hop, first, count):
    def body(info_ref, *refs):
        (local_ref, g_ref, dz_ref, near_ref, far_ref, below_ref, above_ref) = refs[-7:]
        kept_below, kept_above, _ = refs[-10:-7]
        arrays, inputs = refs[-15:-10], refs[:-15]
        odd = odd_of(info_ref) == 1

        def sort(below, above):
            near_ref[...] = jnp.where(odd, below, above)
            far_ref[...] = jnp.where(odd, above, below)

        @pl.when(hop_of(info_ref) == hop)
        def _():
            step(start_values(hop, first, count, inputs), *arrays, local_ref, below_ref, above_ref, g_ref, dz_ref)
            sort(below_ref[...], above_ref[...])

        @pl.when(hop_of(info_ref) != hop)
        def _():
            sort(kept_below[first : first + count], kept_above[first : first + count])

    return body


def gradients(x_ref, parts, out_ref, start=None):
    rows, width = x_ref.shape[1:]
    for n in range(3):
        total = 0.0 if start is None else start[n * width : (n + 1) * width]
        for first, size, agg, act, g, dz in parts:
            left = (x_ref[first : first + size], agg[...] if n == 1 else None, act[...] if n == 2 else None)[n]
            right = g() if n == 2 else dz()
            total = total + dot(left.reshape(size * rows, width), right.reshape(size * rows, width), ((0,), (0,)))
        out_ref[n * width : (n + 1) * width] = total


def make_partial_kernel(hops, chunks):
    def body(info_ref, x_ref, *refs):
        (part_ref, local_ref, below_ref, above_ref, near_ref, far_ref, g_ref, dz_ref, sems) = refs[-9:]
        early = chunks - 1
        forward = [refs[2 * c : 2 * c + 2] for c in range(chunks)]
        here = [refs[2 * chunks + 4 * c : 2 * chunks + 4 * c + 4] for c in range(early)]
        pieces = refs[2 * chunks + 4 * early : -9]
        targets = (local_ref, below_ref, above_ref, g_ref, dz_ref)
        batches = x_ref.shape[0]
        count = batches // chunks
        odd = odd_of(info_ref) == 1

        def copies(hop):
            return [pltpu.make_async_copy(pieces[(hop * chunks + c) * 5 + n],
                                          targets[n].at[pl.ds(c * count, count)], sems.at[n, c])
                    for n in range(5) for c in range(chunks)]

        def sort(below, above, where):
            near_ref[where] = jnp.where(odd, below, above)
            far_ref[where] = jnp.where(odd, above, below)

        for hop in range(hops - 1):
            @pl.when(hop_of(info_ref) == hop)
            def _():
                for copy in copies(hop):
                    copy.start()

        @pl.when(hop_of(info_ref) == hops - 1)
        def _():
            parts = []
            for c, (below, above, g, dz) in enumerate(here):
                sort(below[...], above[...], slice(c * count, (c + 1) * count))
                parts.append((c * count, count, *forward[c], lambda g=g: g[...], lambda dz=dz: dz[...]))
            if parts:
                gradients(x_ref, parts, part_ref)
            else:
                part_ref[...] = jnp.zeros_like(part_ref)

        if hops > 1:
            @pl.when(hop_of(info_ref) != hops - 1)
            def _():
                for copy in copies(0):
                    copy.wait()
                if early:
                    sort(below_ref[: early * count], above_ref[: early * count], slice(0, early * count))
                parts = []
                for c in range(chunks):
                    where = slice(c * count, (c + 1) * count)
                    parts.append((c * count, count, *forward[c], lambda w=where: g_ref[w], lambda w=where: dz_ref[w]))
                gradients(x_ref, parts, part_ref)

    return body


def make_weight_kernel(last, first, count):
    def body(info_ref, x_ref, agg_ref, act_ref, part_ref, g_ref, dz_ref, near_early_ref, near_ref, far_ref,
             keep_ref, give_ref, grad_ref):
        width = part_ref.shape[1]
        half = keep_ref.shape[0]
        odd = odd_of(info_ref)

        @pl.when(hop_of(info_ref) == last)
        def _():
            parts = [(first, count, agg_ref, act_ref, lambda: g_ref[...], lambda: dz_ref[...])]
            gradients(x_ref, parts, grad_ref, part_ref)

        @pl.when(hop_of(info_ref) != last)
        def _():
            grad_ref[...] = part_ref[...]

        keep_ref[...] = grad_ref[pl.ds(pl.multiple_of(odd * half, half), half)]
        give_ref[:half] = grad_ref[pl.ds(pl.multiple_of((1 - odd) * half, half), half)].astype(BF16)
        start = half
        for ref in (near_early_ref, near_ref, far_ref):
            size = ref.shape[0] * ref.shape[1]
            if start < give_ref.shape[0]:
                give_ref[start : start + size] = ref[...].reshape(size, width)
            start += size

    return body


def add(a, b):
    return (a.astype(F32) + b.astype(F32)).astype(BF16)


def take_kernel(keep_ref, came_ref, far_ref, p_ref, q_ref):
    quarter = q_ref.shape[0]
    p_ref[:quarter] = add(keep_ref[:quarter], came_ref[:quarter])
    q_ref[...] = add(keep_ref[quarter:], came_ref[quarter : 2 * quarter])
    extra = p_ref.shape[0] - quarter
    if extra:
        p_ref[quarter:] = came_ref[came_ref.shape[0] - extra :]


def forward_sum_kernel(p_ref, other_ref, out_ref, *, quarter):
    out_ref[:quarter] = add(p_ref[:quarter], other_ref[:quarter])
    out_ref[quarter:] = other_ref[quarter:]


def join_kernel(p_ref, p_other_ref, q_ref, q_other_ref, out_ref):
    quarter = q_ref.shape[0]
    out_ref[:quarter] = add(p_ref[:quarter], p_other_ref[:quarter])
    out_ref[quarter:] = add(q_ref[...], q_other_ref[...])


def half_copies(high, value_ref, first_ref, second_ref, sems):
    half = value_ref.shape[0]
    size = first_ref.shape[0]
    if not high:
        return [pltpu.make_async_copy(value_ref, first_ref.at[pl.ds(0, half)], sems.at[0])]
    return [pltpu.make_async_copy(value_ref.at[pl.ds(0, size - half)], first_ref.at[pl.ds(half, size - half)], sems.at[0]),
            pltpu.make_async_copy(value_ref.at[pl.ds(size - half, 2 * half - size)], second_ref, sems.at[1])]


def for_half(high, act, *refs):
    for case in (0, 1):
        @pl.when(high == case)
        def _():
            for copy in half_copies(case, *refs):
                act(copy)


def split_kernel(info_ref, other_ref, first_in, second_in, first_ref, second_ref, value_ref, sems):
    value_ref[...] = other_ref[...].astype(F32)
    refs = (1 - odd_of(info_ref), value_ref, first_ref, second_ref, sems)
    for_half(refs[0], lambda copy: copy.start(), *refs[1:])
    for_half(refs[0], lambda copy: copy.wait(), *refs[1:])


def make_finish_kernel(last, start, slots, relay):
    def body(info_ref, mine_ref, came_ref, place_ref, far_early_ref, loc_ref, *refs):
        here, halos, (out_ref, first_ref, second_ref, value_ref, sems) = refs[: -6 - relay], refs[-6 - relay : -5], refs[-5:]
        odd, end = odd_of(info_ref) == 1, end_of(info_ref) == 1
        batches = loc_ref.shape[0]
        count = batches // len(here)
        early = batches - count
        value_ref[...] = mine_ref[...].astype(F32)
        half_refs = (value_ref, first_ref, second_ref, sems)
        for_half(odd_of(info_ref), lambda copy: copy.start(), *half_refs)

        def far_of(m):
            if m < early:
                return far_early_ref[m]
            if not relay:
                return halos[0][m - early]
            first, second = [halo[halo.shape[0] - (batches - m) * slots :][:slots] for halo in halos]
            return jnp.where(direct_of(info_ref) == 1, first, second)

        def write(local):
            for m in range(batches):
                near = came_ref[start + m * slots : start + (m + 1) * slots]
                far = far_of(m)
                far = jnp.where(end, jnp.zeros_like(far), far)
                upper = jnp.where(odd, far, near)
                lower = jnp.where(odd, near, far)
                out_ref[m] = assemble(local(m), upper, lower, place_ref[...])

        @pl.when(hop_of(info_ref) == last)
        def _():
            write(lambda m: here[m // count][m % count])

        @pl.when(hop_of(info_ref) != last)
        def _():
            write(lambda m: loc_ref[m])

        for_half(odd_of(info_ref), lambda copy: copy.wait(), *half_refs)

    return body


def per_device(saved_inputs, grad_out, w_first, w_second, face_weight, neighbours, send_rows):
    x = saved_inputs[0]
    w1 = w_first[0]
    w2 = w_second[0]
    batches, rows, width = x.shape
    slots = send_rows.shape[1]
    sections = lax.axis_size("section")
    doms = lax.axis_size("dom")
    chunks = CHUNKS if batches % CHUNKS == 0 else 1
    count = batches // chunks
    dom = lax.axis_index("dom")
    hop_here = sections - 1 - lax.axis_index("section")
    end = ((dom == 0) | (dom == doms - 1)).astype(jnp.int32)
    direct = ((dom + 1) % 4 >= 2).astype(jnp.int32)
    info = (8 * hop_here + 4 * direct + 2 * (dom % 2) + end).astype(jnp.int32).reshape(1)
    sds = jax.ShapeDtypeStruct
    smem = pl.BlockSpec(memory_space=pltpu.SMEM)
    any_spec = pl.BlockSpec(memory_space=pl.ANY)
    hbm_spec = pl.BlockSpec(memory_space=pltpu.HBM)

    def like(value):
        return sds(value.shape, value.dtype)

    def call(body, outs, *args, scratch=(), name):
        return pl.pallas_call(
            body, in_specs=[smem] + [vmem()] * (len(args) - 1), out_specs=[vmem()] * len(outs), out_shape=outs,
            scratch_shapes=scratch, compiler_params=params(), name=name,
        )(*args)

    near_pairs = [(p, p ^ 1) for p in range(doms)]
    far_pairs = [(p, (p + 1 if p % 2 else p - 1) % doms) for p in range(doms)]

    edge_shape = sds((batches, slots, width), BF16)
    x, grad_out, w1, w2, neighbours, face_weight, place, near, far = pl.pallas_call(
        load_kernel,
        in_specs=[smem] + [hbm_spec] * 7,
        out_specs=[vmem()] * 9,
        out_shape=(like(x), like(grad_out), like(w1), like(w2), like(neighbours), like(face_weight),
                   sds((rows, 2 * slots), BF16), edge_shape, edge_shape),
        scratch_shapes=[pltpu.VMEM(send_rows.shape, send_rows.dtype), pltpu.SemaphoreType.DMA((7,))],
        compiler_params=params(), name="load",
    )(info, *[pltpu.with_memory_space_constraint(value, pltpu.HBM)
             for value in (x, grad_out, w1, w2, neighbours, face_weight, send_rows)])
    near, far = lax.ppermute(near, "dom", near_pairs), lax.ppermute(far, "dom", far_pairs)

    full_shape = sds((batches, rows, width), BF16)
    wide_shape = sds((batches, rows, width), F32)
    base, inner, own, halo = pl.pallas_call(
        inner_kernel, in_specs=[vmem()] * 4, out_specs=[vmem()] * 4,
        out_shape=(wide_shape, wide_shape, sds((rows, rows), BF16), sds((2 * slots, rows), BF16)),
        compiler_params=params(), name="inner",
    )(x, neighbours, face_weight, w1)
    forward = []
    for c in range(chunks):
        small = sds((count, rows, width), BF16)
        forward.append(call(
            make_forward_kernel(c * count), (sds(small.shape, F32), small, small),
            info, base, inner, near, far, halo, w1, name="forward"))

    def move(value, hop, shift):
        source = sections - 1 - hop
        pairs = [(p * sections + source, (p + shift) * sections + source - 1)
                 for p in range(doms) if 0 <= p + shift < doms]
        return lax.ppermute(value, ("dom", "section"), pairs)

    piece, piece_edge = sds((count, rows, width), BF16), sds((count, slots, width), BF16)
    estimate = pl.CostEstimate(flops=STEP_FLOPS, bytes_accessed=1 << 20, transcendentals=0)
    pieces = []
    received = [None] * chunks
    weights = (own, halo, w1, w2)
    for hop in range(sections):
        sent = []
        for c in range(chunks):
            inputs = (grad_out,) if hop == 0 else (*received[c], place)
            if hop + 1 == sections and c + 1 == chunks:
                break
            local, to_below, to_above, g, dz = pl.pallas_call(
                make_step_kernel(hop, c * count, count),
                in_specs=[smem] + [vmem()] * (len(inputs) + 5), out_specs=[vmem()] * 5,
                out_shape=(piece, piece_edge, piece_edge, piece, piece),
                cost_estimate=estimate, compiler_params=params(), name="step",
            )(info, *inputs, forward[c][0], *weights)
            pieces.append((local, to_below, to_above, g, dz))
            if hop + 1 < sections:
                sent.append((move(local, hop, 0), move(to_below, hop, -1), move(to_above, hop, 1)))
        received = sent if sent else received

    early = chunks - 1
    here, others = pieces[len(pieces) - early :], pieces[: len(pieces) - early]
    last = sections - 1
    early_shape = sds((max(early * count, 1), slots, width), BF16)
    part, local, kept_below, kept_above, near_early, far_early = pl.pallas_call(
        make_partial_kernel(sections, chunks),
        in_specs=[smem] + [vmem()] * (1 + 2 * chunks + 4 * early) + [any_spec] * (5 * len(others)),
        out_specs=[vmem()] * 6,
        out_shape=(sds((3 * width, width), F32), full_shape, edge_shape, edge_shape, early_shape, early_shape),
        scratch_shapes=[pltpu.VMEM(full_shape.shape, BF16)] * 2 + [pltpu.SemaphoreType.DMA((5, chunks))],
        compiler_params=params(), name="partial",
    )(info, x, *[value for _, act, agg in forward for value in (agg, act)],
      *[value for outs in here for value in outs[1:]], *[value for outs in others for value in outs])
    far_early = lax.ppermute(far_early, "dom", far_pairs)
    local_last, g, dz, near, far = pl.pallas_call(
        make_last_kernel(last, early * count, count),
        in_specs=[smem] + [vmem()] * (len(inputs) + 7) + [any_spec], out_specs=[vmem()] * 5,
        out_shape=(piece, piece, piece, piece_edge, piece_edge),
        scratch_shapes=[pltpu.VMEM(piece_edge.shape, BF16)] * 2,
        cost_estimate=estimate, compiler_params=params(), name="step_last",
    )(info, *inputs, forward[-1][0], *weights, kept_below, kept_above, far_early)
    relay = doms == 8
    half = 3 * width // 2
    near_size, far_size = batches * slots, relay * count * slots
    _, act, agg = forward[-1]
    keep, give = pl.pallas_call(
        make_weight_kernel(last, early * count, count), in_specs=[smem] + [vmem()] * 9, out_specs=[vmem()] * 2,
        out_shape=(sds((half, width), F32), sds((half + near_size + far_size, width), BF16)),
        scratch_shapes=[pltpu.VMEM((3 * width, width), F32)],
        cost_estimate=estimate, compiler_params=params(), name="weights",
    )(info, x, agg, act, part, g, dz, near_early, near, far)
    if not relay:
        far = lax.ppermute(far, "dom", far_pairs)

    def swap(value, mask):
        return lax.ppermute(value, "dom", [(i, i ^ mask) for i in range(doms)])

    came = swap(give, 1)
    quarter = sds((half // 2, width), BF16)
    longer = sds((half // 2 + far_size, width), BF16)
    p, q = pl.pallas_call(
        take_kernel, in_specs=[vmem()] * 2 + [any_spec], out_specs=[vmem()] * 2, out_shape=(longer, quarter),
        compiler_params=params(), name="take",
    )(keep, came, far)
    halos = [] if relay else [far]
    bit = 2
    while bit < doms:
        if bit * 2 < doms:
            p_other, q_other = swap(p, bit), swap(q, 2 * bit)
            if relay:
                halos.append(p_other)
                p = pl.pallas_call(
                    functools.partial(forward_sum_kernel, quarter=half // 2), in_specs=[vmem()] * 2, out_specs=vmem(),
                    out_shape=longer, compiler_params=params(), name="forward_sum",
                )(p, p_other)
            else:
                p = add(p, p_other)
            q = add(q, q_other)
            p_other, q_other = swap(p, 2 * bit), swap(q, bit)
            if relay:
                halos.append(p_other)
        else:
            p_other, q_other = swap(p, bit), swap(q, bit)
        bit *= 4
        if bit < doms:
            p, q = add(p, p_other), add(q, q_other)
    mine = pl.pallas_call(
        join_kernel, in_specs=[vmem()] * 4, out_specs=vmem(), out_shape=sds((half, width), BF16),
        compiler_params=params(), name="join",
    )(p, p_other, q, q_other)
    other = swap(mine, 1)
    outs = (sds((2 * width, width), F32), sds((width, width), F32))
    value = [pltpu.VMEM((half, width), F32), pltpu.SemaphoreType.DMA((2,))]
    grad_in, first, second = pl.pallas_call(
        make_finish_kernel(last, half, slots, relay),
        in_specs=[smem] + [vmem()] * (5 + chunks + len(halos)), out_specs=[vmem()] + [any_spec] * 2,
        out_shape=(full_shape, *outs), scratch_shapes=value, compiler_params=params(), name="finish",
    )(info, mine, came, place, far_early, local, *[outs[0] for outs in here], local_last, *halos)
    first, second = pl.pallas_call(
        split_kernel, in_specs=[smem, vmem(), any_spec, any_spec], out_specs=[any_spec] * 2, out_shape=outs,
        scratch_shapes=value, input_output_aliases={2: 0, 3: 1}, compiler_params=params(), name="split",
    )(info, other, first, second)
    return grad_in[None], first[None], second[None]


def solution(mesh):
    return jax.shard_map(
        per_device,
        mesh=mesh,
        in_specs=(
            P("section", None, "dom", None),
            P(None, "dom", None),
            P("section", None, None),
            P("section", None, None),
            P(None, "dom"),
            P(None, "dom"),
            P(None, "dom"),
        ),
        out_specs=(
            P("section", None, "dom", None),
            P("section", None, None),
            P("section", None, None),
        ),
        check_vma=False,
    )
```

```python
import functools

import jax
import jax.numpy as jnp
from jax import lax
from jax.experimental import pallas as pl
from jax.experimental.pallas import tpu as pltpu
from jax.sharding import PartitionSpec as P

F32 = jnp.float32
BF16 = jnp.bfloat16
CHUNKS = 2
STEP_FLOPS = 2600 * 10**6


def dot(a, b, dims=((1,), (0,))):
    return lax.dot_general(a, b, (dims, ((), ())), preferred_element_type=F32)


def hop_of(info_ref):
    return info_ref[0] >> 3


def direct_of(info_ref):
    return (info_ref[0] >> 2) & 1


def odd_of(info_ref):
    return (info_ref[0] >> 1) & 1


def end_of(info_ref):
    return info_ref[0] & 1


def vmem():
    return pl.BlockSpec(memory_space=pltpu.VMEM)


def params():
    return pltpu.CompilerParams(vmem_limit_bytes=16 * 1024 * 1024)


def load_kernel(info_ref, x_hbm, g_hbm, w1_hbm, w2_hbm, nbr_hbm, coef_hbm, send_hbm,
                x_ref, g_ref, w1_ref, w2_ref, nbr_ref, coef_ref, place_ref, near_ref, far_ref, send_ref, sems):
    sources = (send_hbm, x_hbm, nbr_hbm, coef_hbm, w1_hbm, w2_hbm, g_hbm)
    targets = (send_ref, x_ref, nbr_ref, coef_ref, w1_ref, w2_ref, g_ref)
    copies = [pltpu.make_async_copy(source, target, sems.at[n])
              for n, (source, target) in enumerate(zip(sources, targets))]
    for copy in copies:
        copy.start()
    batches, rows, _ = x_ref.shape
    slots = send_ref.shape[1]
    row = lax.broadcasted_iota(jnp.int32, (rows, slots), 0)
    copies[0].wait()
    up = jnp.where(row == send_ref[0:1, :], 1.0, 0.0)
    down = jnp.where(row == send_ref[1:2, :], 1.0, 0.0)
    place = jnp.concatenate([up, down], axis=1)
    place_ref[...] = place.astype(BF16)
    pick = place.T.astype(BF16)
    copies[1].wait()
    odd = odd_of(info_ref) == 1
    for m in range(batches):
        sent = dot(pick, x_ref[m])
        up, down = sent[:slots], sent[slots:]
        near_ref[m] = jnp.where(odd, down, up).astype(BF16)
        far_ref[m] = jnp.where(odd, up, down).astype(BF16)
    for copy in copies[2:]:
        copy.wait()


def inner_kernel(x_ref, nbr_ref, coef_ref, w_ref, base_ref, inner_ref, own_ref, halo_ref):
    batches, rows, width = x_ref.shape
    slots = halo_ref.shape[0] // 2
    faces = nbr_ref.shape[0]
    slot = lax.broadcasted_iota(jnp.int32, (rows + 2 * slots, rows), 0)
    spread = jnp.zeros((rows + 2 * slots, rows), F32)
    for k in range(faces):
        spread = spread + jnp.where(slot == nbr_ref[k : k + 1, :], coef_ref[k : k + 1, :], 0.0)
    own = spread[slots : slots + rows]
    halo_ref[...] = jnp.concatenate([spread[:slots], spread[slots + rows :]], axis=0).astype(BF16)
    own_ref[...] = own.astype(BF16)
    own_t = own.T.astype(BF16)
    for m in range(batches):
        x = x_ref[m]
        inner_ref[m] = dot(own_t, x)
        base_ref[m] = dot(x, w_ref[:width])


def make_forward_kernel(first):
    def body(info_ref, base_ref, inner_ref, near_ref, far_ref, halo_ref, w_ref, slope_ref, act_ref, agg_ref):
        width = base_ref.shape[2]
        slots = near_ref.shape[1]
        odd = odd_of(info_ref) == 1
        lower, upper = halo_ref[:slots].astype(F32), halo_ref[slots:].astype(F32)
        near = jnp.where(odd, lower, upper)
        far = jnp.where(end_of(info_ref) == 1, 0.0, jnp.where(odd, upper, lower))
        halo_t = jnp.concatenate([near, far], axis=0).T.astype(BF16)
        for j in range(slope_ref.shape[0]):
            m = first + j
            edge = jnp.concatenate([near_ref[m], far_ref[m]], axis=0)
            agg = (inner_ref[m] + dot(halo_t, edge)).astype(BF16)
            z = base_ref[m] + dot(agg, w_ref[width:])
            sig = 1.0 / (1.0 + jnp.exp(-z))
            agg_ref[j] = agg
            act_ref[j] = (z * sig).astype(BF16)
            slope_ref[j] = sig * (1.0 + z * (1.0 - sig))

    return body


def assemble(local, upper, lower, place):
    edge = jnp.concatenate([upper, lower], axis=0)
    return (local.astype(F32) + dot(place, edge)).astype(BF16)


def step(g, slope_ref, own_ref, halo_ref, w1_ref, w2_ref, local_ref, below_ref, above_ref, g_ref, dz_ref):
    rows, width = slope_ref.shape[1:]
    slots = halo_ref.shape[0] // 2
    count = len(g)
    d_act = dot(jnp.concatenate(g, axis=0), w2_ref[...], ((1,), (1,)))
    dz = [(d_act[j * rows : (j + 1) * rows] * slope_ref[j]).astype(BF16) for j in range(count)]
    dj = dot(jnp.concatenate(dz, axis=0), w1_ref[...], ((1,), (1,)))
    for j in range(count):
        part = dj[j * rows : (j + 1) * rows]
        dagg = part[:, width:].astype(BF16)
        local = g[j].astype(F32) + part[:, :width] + dot(own_ref[...], dagg)
        local_ref[j] = local.astype(BF16)
        edge = dot(halo_ref[...], dagg).astype(BF16)
        below_ref[j] = edge[:slots]
        above_ref[j] = edge[slots:]
        g_ref[j] = g[j]
        dz_ref[j] = dz[j]


def start_values(hop, first, count, inputs):
    if hop == 0:
        return [inputs[0][first + j] for j in range(count)]
    loc_ref, upper_ref, lower_ref, place_ref = inputs
    return [assemble(loc_ref[j], upper_ref[j], lower_ref[j], place_ref[...]) for j in range(count)]


def make_step_kernel(hop, first, count):
    def body(info_ref, *refs):
        inputs, arrays = refs[:-10], refs[-10:]

        @pl.when(hop_of(info_ref) == hop)
        def _():
            step(start_values(hop, first, count, inputs), *arrays)

    return body


def make_last_kernel(hop, first, count):
    def body(info_ref, *refs):
        (local_ref, g_ref, dz_ref, near_ref, far_ref, below_ref, above_ref) = refs[-7:]
        kept_below, kept_above, _ = refs[-10:-7]
        arrays, inputs = refs[-15:-10], refs[:-15]
        odd = odd_of(info_ref) == 1

        def sort(below, above):
            near_ref[...] = jnp.where(odd, below, above)
            far_ref[...] = jnp.where(odd, above, below)

        @pl.when(hop_of(info_ref) == hop)
        def _():
            step(start_values(hop, first, count, inputs), *arrays, local_ref, below_ref, above_ref, g_ref, dz_ref)
            sort(below_ref[...], above_ref[...])

        @pl.when(hop_of(info_ref) != hop)
        def _():
            sort(kept_below[first : first + count], kept_above[first : first + count])

    return body


def gradients(x_ref, parts, out_ref, start=None):
    rows, width = x_ref.shape[1:]
    for n in range(3):
        total = 0.0 if start is None else start[n * width : (n + 1) * width]
        for first, size, agg, act, g, dz in parts:
            left = (x_ref[first : first + size], agg[...] if n == 1 else None, act[...] if n == 2 else None)[n]
            right = g() if n == 2 else dz()
            total = total + dot(left.reshape(size * rows, width), right.reshape(size * rows, width), ((0,), (0,)))
        out_ref[n * width : (n + 1) * width] = total


def make_partial_kernel(hops, chunks):
    def body(info_ref, x_ref, *refs):
        (part_ref, local_ref, below_ref, above_ref, near_ref, far_ref, g_ref, dz_ref, sems) = refs[-9:]
        early = chunks - 1
        forward = [refs[2 * c : 2 * c + 2] for c in range(chunks)]
        here = [refs[2 * chunks + 4 * c : 2 * chunks + 4 * c + 4] for c in range(early)]
        pieces = refs[2 * chunks + 4 * early : -9]
        targets = (local_ref, below_ref, above_ref, g_ref, dz_ref)
        batches = x_ref.shape[0]
        count = batches // chunks
        odd = odd_of(info_ref) == 1

        def copies(hop):
            return [pltpu.make_async_copy(pieces[(hop * chunks + c) * 5 + n],
                                          targets[n].at[pl.ds(c * count, count)], sems.at[n, c])
                    for n in range(5) for c in range(chunks)]

        def sort(below, above, where):
            near_ref[where] = jnp.where(odd, below, above)
            far_ref[where] = jnp.where(odd, above, below)

        for hop in range(hops - 1):
            @pl.when(hop_of(info_ref) == hop)
            def _():
                for copy in copies(hop):
                    copy.start()

        @pl.when(hop_of(info_ref) == hops - 1)
        def _():
            parts = []
            for c, (below, above, g, dz) in enumerate(here):
                sort(below[...], above[...], slice(c * count, (c + 1) * count))
                parts.append((c * count, count, *forward[c], lambda g=g: g[...], lambda dz=dz: dz[...]))
            if parts:
                gradients(x_ref, parts, part_ref)
            else:
                part_ref[...] = jnp.zeros_like(part_ref)

        if hops > 1:
            @pl.when(hop_of(info_ref) != hops - 1)
            def _():
                for copy in copies(0):
                    copy.wait()
                if early:
                    sort(below_ref[: early * count], above_ref[: early * count], slice(0, early * count))
                parts = []
                for c in range(chunks):
                    where = slice(c * count, (c + 1) * count)
                    parts.append((c * count, count, *forward[c], lambda w=where: g_ref[w], lambda w=where: dz_ref[w]))
                gradients(x_ref, parts, part_ref)

    return body


def make_weight_kernel(last, first, count):
    def body(info_ref, x_ref, agg_ref, act_ref, part_ref, g_ref, dz_ref, near_early_ref, near_ref, far_ref,
             keep_ref, give_ref, grad_ref):
        width = part_ref.shape[1]
        half = keep_ref.shape[0]
        odd = odd_of(info_ref)

        @pl.when(hop_of(info_ref) == last)
        def _():
            parts = [(first, count, agg_ref, act_ref, lambda: g_ref[...], lambda: dz_ref[...])]
            gradients(x_ref, parts, grad_ref, part_ref)

        @pl.when(hop_of(info_ref) != last)
        def _():
            grad_ref[...] = part_ref[...]

        keep_ref[...] = grad_ref[pl.ds(pl.multiple_of(odd * half, half), half)]
        give_ref[:half] = grad_ref[pl.ds(pl.multiple_of((1 - odd) * half, half), half)].astype(BF16)
        start = half
        for ref in (near_early_ref, near_ref, far_ref):
            size = ref.shape[0] * ref.shape[1]
            if start < give_ref.shape[0]:
                give_ref[start : start + size] = ref[...].reshape(size, width)
            start += size

    return body


def add(a, b):
    return (a.astype(F32) + b.astype(F32)).astype(BF16)


def take_kernel(keep_ref, came_ref, far_ref, p_ref, q_ref):
    quarter = keep_ref.shape[0] // 2
    p_ref[:quarter] = add(keep_ref[:quarter], came_ref[:quarter])
    q_ref[:quarter] = add(keep_ref[quarter:], came_ref[quarter : 2 * quarter])
    extra = p_ref.shape[0] - quarter
    if extra:
        p_ref[quarter:] = came_ref[came_ref.shape[0] - extra :]
        q_ref[quarter:] = came_ref[came_ref.shape[0] - extra :]


def forward_sum_kernel(p_ref, other_ref, out_ref, *, quarter):
    out_ref[:quarter] = add(p_ref[:quarter], other_ref[:quarter])
    out_ref[quarter:] = other_ref[quarter:]


def join_kernel(p_ref, p_other_ref, q_ref, q_other_ref, out_ref):
    quarter = out_ref.shape[0] // 2
    out_ref[:quarter] = add(p_ref[:quarter], p_other_ref[:quarter])
    out_ref[quarter:] = add(q_ref[:quarter], q_other_ref[:quarter])


def half_copies(high, value_ref, first_ref, second_ref, sems):
    half = value_ref.shape[0]
    size = first_ref.shape[0]
    if not high:
        return [pltpu.make_async_copy(value_ref, first_ref.at[pl.ds(0, half)], sems.at[0])]
    return [pltpu.make_async_copy(value_ref.at[pl.ds(0, size - half)], first_ref.at[pl.ds(half, size - half)], sems.at[0]),
            pltpu.make_async_copy(value_ref.at[pl.ds(size - half, 2 * half - size)], second_ref, sems.at[1])]


def for_half(high, act, *refs):
    for case in (0, 1):
        @pl.when(high == case)
        def _():
            for copy in half_copies(case, *refs):
                act(copy)


def split_kernel(info_ref, other_ref, first_in, second_in, first_ref, second_ref, value_ref, sems):
    value_ref[...] = other_ref[...].astype(F32)
    refs = (1 - odd_of(info_ref), value_ref, first_ref, second_ref, sems)
    for_half(refs[0], lambda copy: copy.start(), *refs[1:])
    for_half(refs[0], lambda copy: copy.wait(), *refs[1:])


def make_finish_kernel(last, start, slots, relay):
    def body(info_ref, mine_ref, came_ref, place_ref, far_early_ref, loc_ref, *refs):
        number = 4 if relay else 1
        here, halos, refs = refs[: -5 - number], refs[-5 - number : -5], refs[-5:]
        out_ref, first_ref, second_ref, value_ref, sems = refs
        odd, end = odd_of(info_ref) == 1, end_of(info_ref) == 1
        batches = loc_ref.shape[0]
        count = batches // len(here)
        early = batches - count
        value_ref[...] = mine_ref[...].astype(F32)
        half_refs = (value_ref, first_ref, second_ref, sems)
        for_half(odd_of(info_ref), lambda copy: copy.start(), *half_refs)

        def far_of(m):
            if m < early:
                return far_early_ref[m]
            if not relay:
                return halos[0][m - early]
            rows = [halo[halo.shape[0] - (batches - m) * slots :][:slots] for halo in halos]
            first, second = jnp.where(odd, rows[1], rows[0]), jnp.where(odd, rows[3], rows[2])
            return jnp.where(direct_of(info_ref) == 1, first, second)

        def write(local):
            for m in range(batches):
                near = came_ref[start + m * slots : start + (m + 1) * slots]
                far = far_of(m)
                far = jnp.where(end, jnp.zeros_like(far), far)
                upper = jnp.where(odd, far, near)
                lower = jnp.where(odd, near, far)
                out_ref[m] = assemble(local(m), upper, lower, place_ref[...])

        @pl.when(hop_of(info_ref) == last)
        def _():
            write(lambda m: here[m // count][m % count])

        @pl.when(hop_of(info_ref) != last)
        def _():
            write(lambda m: loc_ref[m])

        for_half(odd_of(info_ref), lambda copy: copy.wait(), *half_refs)

    return body


def per_device(saved_inputs, grad_out, w_first, w_second, face_weight, neighbours, send_rows):
    x = saved_inputs[0]
    w1 = w_first[0]
    w2 = w_second[0]
    batches, rows, width = x.shape
    slots = send_rows.shape[1]
    sections = lax.axis_size("section")
    doms = lax.axis_size("dom")
    chunks = CHUNKS if batches % CHUNKS == 0 else 1
    count = batches // chunks
    dom = lax.axis_index("dom")
    hop_here = sections - 1 - lax.axis_index("section")
    end = ((dom == 0) | (dom == doms - 1)).astype(jnp.int32)
    direct = ((dom + 1) % 4 >= 2).astype(jnp.int32)
    info = (8 * hop_here + 4 * direct + 2 * (dom % 2) + end).astype(jnp.int32).reshape(1)
    sds = jax.ShapeDtypeStruct
    smem = pl.BlockSpec(memory_space=pltpu.SMEM)
    any_spec = pl.BlockSpec(memory_space=pl.ANY)
    hbm_spec = pl.BlockSpec(memory_space=pltpu.HBM)

    def like(value):
        return sds(value.shape, value.dtype)

    def call(body, outs, *args, scratch=(), name):
        return pl.pallas_call(
            body, in_specs=[smem] + [vmem()] * (len(args) - 1), out_specs=[vmem()] * len(outs), out_shape=outs,
            scratch_shapes=scratch, compiler_params=params(), name=name,
        )(*args)

    near_pairs = [(p, p ^ 1) for p in range(doms)]
    far_pairs = [(p, (p + 1 if p % 2 else p - 1) % doms) for p in range(doms)]

    edge_shape = sds((batches, slots, width), BF16)
    x, grad_out, w1, w2, neighbours, face_weight, place, near, far = pl.pallas_call(
        load_kernel,
        in_specs=[smem] + [hbm_spec] * 7,
        out_specs=[vmem()] * 9,
        out_shape=(like(x), like(grad_out), like(w1), like(w2), like(neighbours), like(face_weight),
                   sds((rows, 2 * slots), BF16), edge_shape, edge_shape),
        scratch_shapes=[pltpu.VMEM(send_rows.shape, send_rows.dtype), pltpu.SemaphoreType.DMA((7,))],
        compiler_params=params(), name="load",
    )(info, *[pltpu.with_memory_space_constraint(value, pltpu.HBM)
             for value in (x, grad_out, w1, w2, neighbours, face_weight, send_rows)])
    near, far = lax.ppermute(near, "dom", near_pairs), lax.ppermute(far, "dom", far_pairs)

    full_shape = sds((batches, rows, width), BF16)
    wide_shape = sds((batches, rows, width), F32)
    base, inner, own, halo = pl.pallas_call(
        inner_kernel, in_specs=[vmem()] * 4, out_specs=[vmem()] * 4,
        out_shape=(wide_shape, wide_shape, sds((rows, rows), BF16), sds((2 * slots, rows), BF16)),
        compiler_params=params(), name="inner",
    )(x, neighbours, face_weight, w1)
    forward = []
    for c in range(chunks):
        small = sds((count, rows, width), BF16)
        forward.append(call(
            make_forward_kernel(c * count), (sds(small.shape, F32), small, small),
            info, base, inner, near, far, halo, w1, name="forward"))

    def move(value, hop, shift):
        source = sections - 1 - hop
        pairs = [(p * sections + source, (p + shift) * sections + source - 1)
                 for p in range(doms) if 0 <= p + shift < doms]
        return lax.ppermute(value, ("dom", "section"), pairs)

    piece, piece_edge = sds((count, rows, width), BF16), sds((count, slots, width), BF16)
    estimate = pl.CostEstimate(flops=STEP_FLOPS, bytes_accessed=1 << 20, transcendentals=0)
    pieces = []
    received = [None] * chunks
    weights = (own, halo, w1, w2)
    for hop in range(sections):
        sent = []
        for c in range(chunks):
            inputs = (grad_out,) if hop == 0 else (*received[c], place)
            if hop + 1 == sections and c + 1 == chunks:
                break
            local, to_below, to_above, g, dz = pl.pallas_call(
                make_step_kernel(hop, c * count, count),
                in_specs=[smem] + [vmem()] * (len(inputs) + 5), out_specs=[vmem()] * 5,
                out_shape=(piece, piece_edge, piece_edge, piece, piece),
                cost_estimate=estimate, compiler_params=params(), name="step",
            )(info, *inputs, forward[c][0], *weights)
            pieces.append((local, to_below, to_above, g, dz))
            if hop + 1 < sections:
                sent.append((move(local, hop, 0), move(to_below, hop, -1), move(to_above, hop, 1)))
        received = sent if sent else received

    early = chunks - 1
    here, others = pieces[len(pieces) - early :], pieces[: len(pieces) - early]
    last = sections - 1
    early_shape = sds((max(early * count, 1), slots, width), BF16)
    part, local, kept_below, kept_above, near_early, far_early = pl.pallas_call(
        make_partial_kernel(sections, chunks),
        in_specs=[smem] + [vmem()] * (1 + 2 * chunks + 4 * early) + [any_spec] * (5 * len(others)),
        out_specs=[vmem()] * 6,
        out_shape=(sds((3 * width, width), F32), full_shape, edge_shape, edge_shape, early_shape, early_shape),
        scratch_shapes=[pltpu.VMEM(full_shape.shape, BF16)] * 2 + [pltpu.SemaphoreType.DMA((5, chunks))],
        compiler_params=params(), name="partial",
    )(info, x, *[value for _, act, agg in forward for value in (agg, act)],
      *[value for outs in here for value in outs[1:]], *[value for outs in others for value in outs])
    far_early = lax.ppermute(far_early, "dom", far_pairs)
    local_last, g, dz, near, far = pl.pallas_call(
        make_last_kernel(last, early * count, count),
        in_specs=[smem] + [vmem()] * (len(inputs) + 7) + [any_spec], out_specs=[vmem()] * 5,
        out_shape=(piece, piece, piece, piece_edge, piece_edge),
        scratch_shapes=[pltpu.VMEM(piece_edge.shape, BF16)] * 2,
        cost_estimate=estimate, compiler_params=params(), name="step_last",
    )(info, *inputs, forward[-1][0], *weights, kept_below, kept_above, far_early)
    relay = doms == 8
    half = 3 * width // 2
    near_size, far_size = batches * slots, relay * count * slots
    _, act, agg = forward[-1]
    keep, give = pl.pallas_call(
        make_weight_kernel(last, early * count, count), in_specs=[smem] + [vmem()] * 9, out_specs=[vmem()] * 2,
        out_shape=(sds((half, width), F32), sds((half + near_size + far_size, width), BF16)),
        scratch_shapes=[pltpu.VMEM((3 * width, width), F32)],
        cost_estimate=estimate, compiler_params=params(), name="weights",
    )(info, x, agg, act, part, g, dz, near_early, near, far)
    if not relay:
        far = lax.ppermute(far, "dom", far_pairs)

    def swap(value, mask):
        return lax.ppermute(value, "dom", [(i, i ^ mask) for i in range(doms)])

    came = swap(give, 1)
    longer = sds((half // 2 + far_size, width), BF16)
    p, q = pl.pallas_call(
        take_kernel, in_specs=[vmem()] * 2 + [any_spec], out_specs=[vmem()] * 2, out_shape=(longer, longer),
        compiler_params=params(), name="take",
    )(keep, came, far)
    halos = [] if relay else [far]

    def cross(value, even, odd):
        return lax.ppermute(value, "dom", [(i, i ^ (odd if i % 2 else even)) for i in range(doms)])

    def forward_sum(value, other):
        if not relay:
            return add(value, other)
        return pl.pallas_call(
            functools.partial(forward_sum_kernel, quarter=half // 2), in_specs=[vmem()] * 2, out_specs=vmem(),
            out_shape=longer, compiler_params=params(), name="forward_sum",
        )(value, other)

    bit = 2
    while bit < doms:
        if bit * 2 < doms:
            p_other, q_other = cross(p, bit, 2 * bit), cross(q, 2 * bit, bit)
            if relay:
                halos += [p_other, q_other]
            p, q = forward_sum(p, p_other), forward_sum(q, q_other)
            p_other, q_other = cross(p, 2 * bit, bit), cross(q, bit, 2 * bit)
            if relay:
                halos += [p_other, q_other]
        else:
            p_other, q_other = swap(p, bit), swap(q, bit)
        bit *= 4
        if bit < doms:
            p, q = add(p, p_other), add(q, q_other)
    mine = pl.pallas_call(
        join_kernel, in_specs=[vmem()] * 4, out_specs=vmem(), out_shape=sds((half, width), BF16),
        compiler_params=params(), name="join",
    )(p, p_other, q, q_other)
    other = swap(mine, 1)
    outs = (sds((2 * width, width), F32), sds((width, width), F32))
    value = [pltpu.VMEM((half, width), F32), pltpu.SemaphoreType.DMA((2,))]
    grad_in, first, second = pl.pallas_call(
        make_finish_kernel(last, half, slots, relay),
        in_specs=[smem] + [vmem()] * (5 + chunks + len(halos)), out_specs=[vmem()] + [any_spec] * 2,
        out_shape=(full_shape, *outs), scratch_shapes=value, compiler_params=params(), name="finish",
    )(info, mine, came, place, far_early, local, *[outs[0] for outs in here], local_last, *halos)
    first, second = pl.pallas_call(
        split_kernel, in_specs=[smem, vmem(), any_spec, any_spec], out_specs=[any_spec] * 2, out_shape=outs,
        scratch_shapes=value, input_output_aliases={2: 0, 3: 1}, compiler_params=params(), name="split",
    )(info, other, first, second)
    return grad_in[None], first[None], second[None]


def solution(mesh):
    return jax.shard_map(
        per_device,
        mesh=mesh,
        in_specs=(
            P("section", None, "dom", None),
            P(None, "dom", None),
            P("section", None, None),
            P("section", None, None),
            P(None, "dom"),
            P(None, "dom"),
            P(None, "dom"),
        ),
        out_specs=(
            P("section", None, "dom", None),
            P("section", None, None),
            P("section", None, None),
        ),
        check_vma=False,
    )
```

```python
import functools

import jax
import jax.numpy as jnp
from jax import lax
from jax.experimental import pallas as pl
from jax.experimental.pallas import tpu as pltpu
from jax.sharding import PartitionSpec as P

F32 = jnp.float32
BF16 = jnp.bfloat16
CHUNKS = 2
STEP_FLOPS = 2600 * 10**6


def dot(a, b, dims=((1,), (0,))):
    return lax.dot_general(a, b, (dims, ((), ())), preferred_element_type=F32)


def hop_of(info_ref):
    return info_ref[0] >> 3


def direct_of(info_ref):
    return (info_ref[0] >> 2) & 1


def odd_of(info_ref):
    return (info_ref[0] >> 1) & 1


def end_of(info_ref):
    return info_ref[0] & 1


def vmem():
    return pl.BlockSpec(memory_space=pltpu.VMEM)


def params():
    return pltpu.CompilerParams(vmem_limit_bytes=16 * 1024 * 1024)


def start_all(sources, targets, sems):
    copies = [pltpu.make_async_copy(source, target, sems.at[n])
              for n, (source, target) in enumerate(zip(sources, targets))]
    for copy in copies:
        copy.start()
    return copies


def load_kernel(info_ref, x_hbm, send_hbm, x_ref, place_ref, near_ref, far_ref, send_ref, sems):
    copies = start_all((send_hbm, x_hbm), (send_ref, x_ref), sems)
    batches, rows, _ = x_ref.shape
    slots = send_ref.shape[1]
    row = lax.broadcasted_iota(jnp.int32, (rows, slots), 0)
    copies[0].wait()
    up = jnp.where(row == send_ref[0:1, :], 1.0, 0.0)
    down = jnp.where(row == send_ref[1:2, :], 1.0, 0.0)
    place = jnp.concatenate([up, down], axis=1)
    place_ref[...] = place.astype(BF16)
    pick = place.T.astype(BF16)
    copies[1].wait()
    odd = odd_of(info_ref) == 1
    for m in range(batches):
        sent = dot(pick, x_ref[m])
        up, down = sent[:slots], sent[slots:]
        near_ref[m] = jnp.where(odd, down, up).astype(BF16)
        far_ref[m] = jnp.where(odd, up, down).astype(BF16)


def inner_kernel(x_ref, g_hbm, w1_hbm, w2_hbm, nbr_hbm, coef_hbm,
                 base_ref, inner_ref, own_ref, halo_ref, g_ref, w_ref, w2_ref, nbr_ref, coef_ref, sems):
    copies = start_all((nbr_hbm, coef_hbm, w1_hbm, w2_hbm, g_hbm), (nbr_ref, coef_ref, w_ref, w2_ref, g_ref), sems)
    for copy in copies[:2]:
        copy.wait()
    batches, rows, width = x_ref.shape
    slots = halo_ref.shape[0] // 2
    faces = nbr_ref.shape[0]
    slot = lax.broadcasted_iota(jnp.int32, (rows + 2 * slots, rows), 0)
    spread = jnp.zeros((rows + 2 * slots, rows), F32)
    for k in range(faces):
        spread = spread + jnp.where(slot == nbr_ref[k : k + 1, :], coef_ref[k : k + 1, :], 0.0)
    own = spread[slots : slots + rows]
    halo_ref[...] = jnp.concatenate([spread[:slots], spread[slots + rows :]], axis=0).astype(BF16)
    own_ref[...] = own.astype(BF16)
    own_t = own.T.astype(BF16)
    for copy in copies[2:]:
        copy.wait()
    for m in range(batches):
        x = x_ref[m]
        inner_ref[m] = dot(own_t, x)
        base_ref[m] = dot(x, w_ref[:width])


def make_forward_kernel(first):
    def body(info_ref, base_ref, inner_ref, near_ref, far_ref, halo_ref, w_ref, slope_ref, act_ref, agg_ref):
        width = base_ref.shape[2]
        slots = near_ref.shape[1]
        odd = odd_of(info_ref) == 1
        lower, upper = halo_ref[:slots].astype(F32), halo_ref[slots:].astype(F32)
        near = jnp.where(odd, lower, upper)
        far = jnp.where(end_of(info_ref) == 1, 0.0, jnp.where(odd, upper, lower))
        halo_t = jnp.concatenate([near, far], axis=0).T.astype(BF16)
        for j in range(slope_ref.shape[0]):
            m = first + j
            edge = jnp.concatenate([near_ref[m], far_ref[m]], axis=0)
            agg = (inner_ref[m] + dot(halo_t, edge)).astype(BF16)
            z = base_ref[m] + dot(agg, w_ref[width:])
            sig = 1.0 / (1.0 + jnp.exp(-z))
            agg_ref[j] = agg
            act_ref[j] = (z * sig).astype(BF16)
            slope_ref[j] = sig * (1.0 + z * (1.0 - sig))

    return body


def assemble(local, upper, lower, place):
    edge = jnp.concatenate([upper, lower], axis=0)
    return (local.astype(F32) + dot(place, edge)).astype(BF16)


def step(g, slope_ref, own_ref, halo_ref, w1_ref, w2_ref, local_ref, below_ref, above_ref, g_ref, dz_ref):
    rows, width = slope_ref.shape[1:]
    slots = halo_ref.shape[0] // 2
    count = len(g)
    d_act = dot(jnp.concatenate(g, axis=0), w2_ref[...], ((1,), (1,)))
    dz = [(d_act[j * rows : (j + 1) * rows] * slope_ref[j]).astype(BF16) for j in range(count)]
    dj = dot(jnp.concatenate(dz, axis=0), w1_ref[...], ((1,), (1,)))
    for j in range(count):
        part = dj[j * rows : (j + 1) * rows]
        dagg = part[:, width:].astype(BF16)
        local = g[j].astype(F32) + part[:, :width] + dot(own_ref[...], dagg)
        local_ref[j] = local.astype(BF16)
        edge = dot(halo_ref[...], dagg).astype(BF16)
        below_ref[j] = edge[:slots]
        above_ref[j] = edge[slots:]
        g_ref[j] = g[j]
        dz_ref[j] = dz[j]


def start_values(hop, first, count, inputs):
    if hop == 0:
        return [inputs[0][first + j] for j in range(count)]
    loc_ref, upper_ref, lower_ref, place_ref = inputs
    return [assemble(loc_ref[j], upper_ref[j], lower_ref[j], place_ref[...]) for j in range(count)]


def make_step_kernel(hop, first, count):
    def body(info_ref, *refs):
        inputs, arrays = refs[:-10], refs[-10:]

        @pl.when(hop_of(info_ref) == hop)
        def _():
            step(start_values(hop, first, count, inputs), *arrays)

    return body


def make_last_kernel(hop, first, count):
    def body(info_ref, *refs):
        (local_ref, g_ref, dz_ref, near_ref, far_ref, below_ref, above_ref) = refs[-7:]
        kept_below, kept_above, _ = refs[-10:-7]
        arrays, inputs = refs[-15:-10], refs[:-15]
        odd = odd_of(info_ref) == 1

        def sort(below, above):
            near_ref[...] = jnp.where(odd, below, above)
            far_ref[...] = jnp.where(odd, above, below)

        @pl.when(hop_of(info_ref) == hop)
        def _():
            step(start_values(hop, first, count, inputs), *arrays, local_ref, below_ref, above_ref, g_ref, dz_ref)
            sort(below_ref[...], above_ref[...])

        @pl.when(hop_of(info_ref) != hop)
        def _():
            sort(kept_below[first : first + count], kept_above[first : first + count])

    return body


def gradients(x_ref, parts, out_ref, start=None):
    rows, width = x_ref.shape[1:]
    for n in range(3):
        total = 0.0 if start is None else start[n * width : (n + 1) * width]
        for first, size, agg, act, g, dz in parts:
            left = (x_ref[first : first + size], agg[...] if n == 1 else None, act[...] if n == 2 else None)[n]
            right = g() if n == 2 else dz()
            total = total + dot(left.reshape(size * rows, width), right.reshape(size * rows, width), ((0,), (0,)))
        out_ref[n * width : (n + 1) * width] = total


def make_partial_kernel(hops, chunks):
    def body(info_ref, x_ref, *refs):
        (part_ref, local_ref, below_ref, above_ref, near_ref, far_ref, g_ref, dz_ref, sems) = refs[-9:]
        early = chunks - 1
        forward = [refs[2 * c : 2 * c + 2] for c in range(chunks)]
        here = [refs[2 * chunks + 4 * c : 2 * chunks + 4 * c + 4] for c in range(early)]
        pieces = refs[2 * chunks + 4 * early : -9]
        targets = (local_ref, below_ref, above_ref, g_ref, dz_ref)
        batches = x_ref.shape[0]
        count = batches // chunks
        odd = odd_of(info_ref) == 1

        def copies(hop):
            return [pltpu.make_async_copy(pieces[(hop * chunks + c) * 5 + n],
                                          targets[n].at[pl.ds(c * count, count)], sems.at[n, c])
                    for n in range(5) for c in range(chunks)]

        def sort(below, above, where):
            near_ref[where] = jnp.where(odd, below, above)
            far_ref[where] = jnp.where(odd, above, below)

        for hop in range(hops - 1):
            @pl.when(hop_of(info_ref) == hop)
            def _():
                for copy in copies(hop):
                    copy.start()

        @pl.when(hop_of(info_ref) == hops - 1)
        def _():
            parts = []
            for c, (below, above, g, dz) in enumerate(here):
                sort(below[...], above[...], slice(c * count, (c + 1) * count))
                parts.append((c * count, count, *forward[c], lambda g=g: g[...], lambda dz=dz: dz[...]))
            if parts:
                gradients(x_ref, parts, part_ref)
            else:
                part_ref[...] = jnp.zeros_like(part_ref)

        if hops > 1:
            @pl.when(hop_of(info_ref) != hops - 1)
            def _():
                for copy in copies(0):
                    copy.wait()
                if early:
                    sort(below_ref[: early * count], above_ref[: early * count], slice(0, early * count))
                parts = []
                for c in range(chunks):
                    where = slice(c * count, (c + 1) * count)
                    parts.append((c * count, count, *forward[c], lambda w=where: g_ref[w], lambda w=where: dz_ref[w]))
                gradients(x_ref, parts, part_ref)

    return body


def make_weight_kernel(last, first, count):
    def body(info_ref, x_ref, agg_ref, act_ref, part_ref, g_ref, dz_ref, near_early_ref, near_ref, far_ref,
             keep_ref, give_ref, grad_ref):
        width = part_ref.shape[1]
        half = keep_ref.shape[0]
        odd = odd_of(info_ref)

        @pl.when(hop_of(info_ref) == last)
        def _():
            parts = [(first, count, agg_ref, act_ref, lambda: g_ref[...], lambda: dz_ref[...])]
            gradients(x_ref, parts, grad_ref, part_ref)

        @pl.when(hop_of(info_ref) != last)
        def _():
            grad_ref[...] = part_ref[...]

        keep_ref[...] = grad_ref[pl.ds(pl.multiple_of(odd * half, half), half)]
        give_ref[:half] = grad_ref[pl.ds(pl.multiple_of((1 - odd) * half, half), half)].astype(BF16)
        start = half
        for ref in (near_early_ref, near_ref, far_ref):
            size = ref.shape[0] * ref.shape[1]
            if start < give_ref.shape[0]:
                give_ref[start : start + size] = ref[...].reshape(size, width)
            start += size

    return body


def add(a, b):
    return (a.astype(F32) + b.astype(F32)).astype(BF16)


def take_kernel(keep_ref, came_ref, far_ref, p_ref, q_ref):
    quarter = keep_ref.shape[0] // 2
    p_ref[:quarter] = add(keep_ref[:quarter], came_ref[:quarter])
    q_ref[:quarter] = add(keep_ref[quarter:], came_ref[quarter : 2 * quarter])
    extra = p_ref.shape[0] - quarter
    if extra:
        p_ref[quarter:] = came_ref[came_ref.shape[0] - extra :]
        q_ref[quarter:] = came_ref[came_ref.shape[0] - extra :]


def forward_sum_kernel(p_ref, other_ref, out_ref, *, quarter):
    out_ref[:quarter] = add(p_ref[:quarter], other_ref[:quarter])
    out_ref[quarter:] = other_ref[quarter:]


def join_kernel(p_ref, p_other_ref, q_ref, q_other_ref, out_ref):
    quarter = out_ref.shape[0] // 2
    out_ref[:quarter] = add(p_ref[:quarter], p_other_ref[:quarter])
    out_ref[quarter:] = add(q_ref[:quarter], q_other_ref[:quarter])


def half_copies(high, value_ref, first_ref, second_ref, sems):
    half = value_ref.shape[0]
    size = first_ref.shape[0]
    if not high:
        return [pltpu.make_async_copy(value_ref, first_ref.at[pl.ds(0, half)], sems.at[0])]
    return [pltpu.make_async_copy(value_ref.at[pl.ds(0, size - half)], first_ref.at[pl.ds(half, size - half)], sems.at[0]),
            pltpu.make_async_copy(value_ref.at[pl.ds(size - half, 2 * half - size)], second_ref, sems.at[1])]


def for_half(high, act, *refs):
    for case in (0, 1):
        @pl.when(high == case)
        def _():
            for copy in half_copies(case, *refs):
                act(copy)


def split_kernel(info_ref, other_ref, first_in, second_in, first_ref, second_ref, value_ref, sems):
    value_ref[...] = other_ref[...].astype(F32)
    refs = (1 - odd_of(info_ref), value_ref, first_ref, second_ref, sems)
    for_half(refs[0], lambda copy: copy.start(), *refs[1:])
    for_half(refs[0], lambda copy: copy.wait(), *refs[1:])


def make_finish_kernel(last, start, slots, relay):
    def body(info_ref, mine_ref, came_ref, place_ref, far_early_ref, loc_ref, *refs):
        number = 4 if relay else 1
        here, halos, refs = refs[: -7 - number], refs[-7 - number : -7], refs[-7:]
        out_ref, first_ref, second_ref, value_ref, sems, rows_ref, row_sems = refs
        odd, end = odd_of(info_ref) == 1, end_of(info_ref) == 1
        batches = loc_ref.shape[0]
        count = batches // len(here)
        early = batches - count
        value_ref[...] = mine_ref[...].astype(F32)
        half_refs = (value_ref, first_ref, second_ref, sems)
        for_half(odd_of(info_ref), lambda copy: copy.start(), *half_refs)

        def far_of(m):
            if m < early:
                return far_early_ref[m]
            if not relay:
                return halos[0][m - early]
            rows = [halo[halo.shape[0] - (batches - m) * slots :][:slots] for halo in halos]
            first, second = jnp.where(odd, rows[1], rows[0]), jnp.where(odd, rows[3], rows[2])
            return jnp.where(direct_of(info_ref) == 1, first, second)

        def write(local):
            for m in range(batches):
                near = came_ref[start + m * slots : start + (m + 1) * slots]
                far = far_of(m)
                far = jnp.where(end, jnp.zeros_like(far), far)
                upper = jnp.where(odd, far, near)
                lower = jnp.where(odd, near, far)
                rows_ref[m] = assemble(local(m), upper, lower, place_ref[...])
                row_copy(m).start()

        def row_copy(m):
            return pltpu.make_async_copy(rows_ref.at[m], out_ref.at[m], row_sems.at[m])

        @pl.when(hop_of(info_ref) == last)
        def _():
            write(lambda m: here[m // count][m % count])

        @pl.when(hop_of(info_ref) != last)
        def _():
            write(lambda m: loc_ref[m])

        for m in range(batches):
            row_copy(m).wait()
        for_half(odd_of(info_ref), lambda copy: copy.wait(), *half_refs)

    return body


def per_device(saved_inputs, grad_out, w_first, w_second, face_weight, neighbours, send_rows):
    x = saved_inputs[0]
    w1 = w_first[0]
    w2 = w_second[0]
    batches, rows, width = x.shape
    slots = send_rows.shape[1]
    sections = lax.axis_size("section")
    doms = lax.axis_size("dom")
    chunks = CHUNKS if batches % CHUNKS == 0 else 1
    count = batches // chunks
    dom = lax.axis_index("dom")
    hop_here = sections - 1 - lax.axis_index("section")
    end = ((dom == 0) | (dom == doms - 1)).astype(jnp.int32)
    direct = ((dom + 1) % 4 >= 2).astype(jnp.int32)
    info = (8 * hop_here + 4 * direct + 2 * (dom % 2) + end).astype(jnp.int32).reshape(1)
    sds = jax.ShapeDtypeStruct
    smem = pl.BlockSpec(memory_space=pltpu.SMEM)
    any_spec = pl.BlockSpec(memory_space=pl.ANY)
    hbm_spec = pl.BlockSpec(memory_space=pltpu.HBM)

    def like(value):
        return sds(value.shape, value.dtype)

    def call(body, outs, *args, scratch=(), name):
        return pl.pallas_call(
            body, in_specs=[smem] + [vmem()] * (len(args) - 1), out_specs=[vmem()] * len(outs), out_shape=outs,
            scratch_shapes=scratch, compiler_params=params(), name=name,
        )(*args)

    near_pairs = [(p, p ^ 1) for p in range(doms)]
    far_pairs = [(p, (p + 1 if p % 2 else p - 1) % doms) for p in range(doms)]

    edge_shape = sds((batches, slots, width), BF16)
    def in_hbm(*values):
        return [pltpu.with_memory_space_constraint(value, pltpu.HBM) for value in values]

    x, place, near, far = pl.pallas_call(
        load_kernel, in_specs=[smem] + [hbm_spec] * 2, out_specs=[vmem()] * 4,
        out_shape=(like(x), sds((rows, 2 * slots), BF16), edge_shape, edge_shape),
        scratch_shapes=[pltpu.VMEM(send_rows.shape, send_rows.dtype), pltpu.SemaphoreType.DMA((2,))],
        compiler_params=params(), name="load",
    )(info, *in_hbm(x, send_rows))
    near, far = lax.ppermute(near, "dom", near_pairs), lax.ppermute(far, "dom", far_pairs)

    full_shape = sds((batches, rows, width), BF16)
    wide_shape = sds((batches, rows, width), F32)
    base, inner, own, halo, grad_out, w1, w2 = pl.pallas_call(
        inner_kernel, in_specs=[vmem()] + [hbm_spec] * 5, out_specs=[vmem()] * 7,
        out_shape=(wide_shape, wide_shape, sds((rows, rows), BF16), sds((2 * slots, rows), BF16),
                   like(grad_out), like(w1), like(w2)),
        scratch_shapes=[pltpu.VMEM(neighbours.shape, neighbours.dtype), pltpu.VMEM(face_weight.shape, face_weight.dtype),
                        pltpu.SemaphoreType.DMA((5,))],
        compiler_params=params(), name="inner",
    )(x, *in_hbm(grad_out, w1, w2, neighbours, face_weight))
    forward = []
    for c in range(chunks):
        small = sds((count, rows, width), BF16)
        forward.append(call(
            make_forward_kernel(c * count), (sds(small.shape, F32), small, small),
            info, base, inner, near, far, halo, w1, name="forward"))

    def move(value, hop, shift):
        source = sections - 1 - hop
        pairs = [(p * sections + source, (p + shift) * sections + source - 1)
                 for p in range(doms) if 0 <= p + shift < doms]
        return lax.ppermute(value, ("dom", "section"), pairs)

    piece, piece_edge = sds((count, rows, width), BF16), sds((count, slots, width), BF16)
    estimate = pl.CostEstimate(flops=STEP_FLOPS, bytes_accessed=1 << 20, transcendentals=0)
    pieces = []
    received = [None] * chunks
    weights = (own, halo, w1, w2)
    for hop in range(sections):
        sent = []
        for c in range(chunks):
            inputs = (grad_out,) if hop == 0 else (*received[c], place)
            if hop + 1 == sections and c + 1 == chunks:
                break
            local, to_below, to_above, g, dz = pl.pallas_call(
                make_step_kernel(hop, c * count, count),
                in_specs=[smem] + [vmem()] * (len(inputs) + 5), out_specs=[vmem()] * 5,
                out_shape=(piece, piece_edge, piece_edge, piece, piece),
                cost_estimate=estimate, compiler_params=params(), name="step",
            )(info, *inputs, forward[c][0], *weights)
            pieces.append((local, to_below, to_above, g, dz))
            if hop + 1 < sections:
                sent.append((move(local, hop, 0), move(to_below, hop, -1), move(to_above, hop, 1)))
        received = sent if sent else received

    early = chunks - 1
    here, others = pieces[len(pieces) - early :], pieces[: len(pieces) - early]
    last = sections - 1
    early_shape = sds((max(early * count, 1), slots, width), BF16)
    part, local, kept_below, kept_above, near_early, far_early = pl.pallas_call(
        make_partial_kernel(sections, chunks),
        in_specs=[smem] + [vmem()] * (1 + 2 * chunks + 4 * early) + [any_spec] * (5 * len(others)),
        out_specs=[vmem()] * 6,
        out_shape=(sds((3 * width, width), F32), full_shape, edge_shape, edge_shape, early_shape, early_shape),
        scratch_shapes=[pltpu.VMEM(full_shape.shape, BF16)] * 2 + [pltpu.SemaphoreType.DMA((5, chunks))],
        compiler_params=params(), name="partial",
    )(info, x, *[value for _, act, agg in forward for value in (agg, act)],
      *[value for outs in here for value in outs[1:]], *[value for outs in others for value in outs])
    far_early = lax.ppermute(far_early, "dom", far_pairs)
    local_last, g, dz, near, far = pl.pallas_call(
        make_last_kernel(last, early * count, count),
        in_specs=[smem] + [vmem()] * (len(inputs) + 7) + [any_spec], out_specs=[vmem()] * 5,
        out_shape=(piece, piece, piece, piece_edge, piece_edge),
        scratch_shapes=[pltpu.VMEM(piece_edge.shape, BF16)] * 2,
        cost_estimate=estimate, compiler_params=params(), name="step_last",
    )(info, *inputs, forward[-1][0], *weights, kept_below, kept_above, far_early)
    relay = doms == 8
    half = 3 * width // 2
    near_size, far_size = batches * slots, relay * count * slots
    _, act, agg = forward[-1]
    keep, give = pl.pallas_call(
        make_weight_kernel(last, early * count, count), in_specs=[smem] + [vmem()] * 9, out_specs=[vmem()] * 2,
        out_shape=(sds((half, width), F32), sds((half + near_size + far_size, width), BF16)),
        scratch_shapes=[pltpu.VMEM((3 * width, width), F32)],
        cost_estimate=estimate, compiler_params=params(), name="weights",
    )(info, x, agg, act, part, g, dz, near_early, near, far)
    if not relay:
        far = lax.ppermute(far, "dom", far_pairs)

    def swap(value, mask):
        return lax.ppermute(value, "dom", [(i, i ^ mask) for i in range(doms)])

    came = swap(give, 1)
    longer = sds((half // 2 + far_size, width), BF16)
    p, q = pl.pallas_call(
        take_kernel, in_specs=[vmem()] * 2 + [any_spec], out_specs=[vmem()] * 2, out_shape=(longer, longer),
        compiler_params=params(), name="take",
    )(keep, came, far)
    halos = [] if relay else [far]

    def cross(value, even, odd):
        return lax.ppermute(value, "dom", [(i, i ^ (odd if i % 2 else even)) for i in range(doms)])

    def forward_sum(value, other):
        if not relay:
            return add(value, other)
        return pl.pallas_call(
            functools.partial(forward_sum_kernel, quarter=half // 2), in_specs=[vmem()] * 2, out_specs=vmem(),
            out_shape=longer, compiler_params=params(), name="forward_sum",
        )(value, other)

    bit = 2
    while bit < doms:
        if bit * 2 < doms:
            p_other, q_other = cross(p, bit, 2 * bit), cross(q, 2 * bit, bit)
            if relay:
                halos += [p_other, q_other]
            p, q = forward_sum(p, p_other), forward_sum(q, q_other)
            p_other, q_other = cross(p, 2 * bit, bit), cross(q, bit, 2 * bit)
            if relay:
                halos += [p_other, q_other]
        else:
            p_other, q_other = swap(p, bit), swap(q, bit)
        bit *= 4
        if bit < doms:
            p, q = add(p, p_other), add(q, q_other)
    mine = pl.pallas_call(
        join_kernel, in_specs=[vmem()] * 4, out_specs=vmem(), out_shape=sds((half, width), BF16),
        compiler_params=params(), name="join",
    )(p, p_other, q, q_other)
    other = swap(mine, 1)
    outs = (sds((2 * width, width), F32), sds((width, width), F32))
    value = [pltpu.VMEM((half, width), F32), pltpu.SemaphoreType.DMA((2,))]
    grad_in, first, second = pl.pallas_call(
        make_finish_kernel(last, half, slots, relay),
        in_specs=[smem] + [vmem()] * (5 + chunks + len(halos)), out_specs=[any_spec] * 3,
        out_shape=(full_shape, *outs),
        scratch_shapes=value + [pltpu.VMEM(full_shape.shape, BF16), pltpu.SemaphoreType.DMA((batches,))], compiler_params=params(), name="finish",
    )(info, mine, came, place, far_early, local, *[outs[0] for outs in here], local_last, *halos)
    first, second = pl.pallas_call(
        split_kernel, in_specs=[smem, vmem(), any_spec, any_spec], out_specs=[any_spec] * 2, out_shape=outs,
        scratch_shapes=value, input_output_aliases={2: 0, 3: 1}, compiler_params=params(), name="split",
    )(info, other, first, second)
    return grad_in[None], first[None], second[None]


def solution(mesh):
    return jax.shard_map(
        per_device,
        mesh=mesh,
        in_specs=(
            P("section", None, "dom", None),
            P(None, "dom", None),
            P("section", None, None),
            P("section", None, None),
            P(None, "dom"),
            P(None, "dom"),
            P(None, "dom"),
        ),
        out_specs=(
            P("section", None, "dom", None),
            P("section", None, None),
            P("section", None, None),
        ),
        check_vma=False,
    )
```
